128 devices in a mesh: grp: 4 (over y), sfc: 32 (over z, x, core).
Axes of the slice: x: 4, y: 4, z: 4, core: 2. Of those that a mesh axis runs over, the one named last changes fastest.
Arguments:
- flow_fields: float32 [4, 5, 8192, 128], P('grp', None, 'sfc'), may hold values from -6 to 6
- mean_velocity: float32 [4, 3, 8192, 128], P('grp', None, 'sfc'), may hold values from -3 to 3
- cell_eddy_viscosity: float32 [4, 8192, 128], P('grp', 'sfc'), may hold values from 0.01 to 0.08
- tile_links: int32 [4, 4, 8192], P('grp', None, 'sfc'), may hold values from -1 to 8191, as said below
- tile_target: int32 [4, 8192], P('grp', 'sfc'), may hold values from 0 to 8191, as said below
- projector: float32 [64, 128], replicated, may hold values from -0.5 to 0.5
- acoustic_state: float32 [4, 4, 64, 8192], P('grp', None, None, 'sfc'), may hold values from -6 to 6
- element_face_neighbours: int32 [4, 6, 8192], P('grp', None, 'sfc'), may hold values from -1 to 8191, as said below
- face_codes: int32 [4, 6, 8192], P('grp', None, 'sfc'), may hold values from 0 to 3
Outputs:
- flow_out: float32 [4, 5, 8192, 128], P('grp', None, 'sfc')
- mean_velocity_output: float32 [4, 3, 8192, 128], P('grp', None, 'sfc')
- acoustic_out: float32 [4, 4, 64, 8192], P('grp', None, None, 'sfc')
The draws below stay inside these ranges and needn't reach their ends.
Inputs may be any that keep to these rules, and one draw needn't show every extreme that they name: `tile_links`: each entry is -1 or a tile of the same grp index whose position differs from the tile's own by at most 16. `tile_target`: element e lies on acoustic device e // 256. A tile held at sfc index s targets an element of acoustic device s or s + 1; one flow device sends at most 160 tiles to device s + 1, and in every draw some flow device sends exactly 160. Entries of grp index 3 are not read. `element_face_neighbours`: each entry is -1 or an element whose index differs from the element's own by at most 16.
All inputs are finite; a program needn't handle non-finite values.
Results may differ from the reference program's by a relative error of at most 0.0008.
Values may be sent and summed in bfloat16 or wider, within the bound.
A program may use at most 128 MiB of HBM per device.

```python
import math
import jax
import jax.numpy as jnp
import numpy as np
from jax import lax

FT = 256
CELLS = 128
HW = 16
E_DEV = 256
HE = 16
NP = 64
TILES = 8192
ELEMS = 8192
CAP = 160
N_GRP = 4
N_SFC = 32


def draw_tile_links(key, part):
    positions = jnp.arange(TILES, dtype=jnp.int32)
    reach = jax.random.randint(jax.random.fold_in(key, 11), (N_GRP, 4, TILES), 1, HW + 1)
    sign = jax.random.randint(jax.random.fold_in(key, 12), (N_GRP, 4, TILES), 0, 2) * 2 - 1
    trial_option = positions[None, None, :] + reach * sign
    return jnp.where((trial_option < 0) | (trial_option >= TILES), -1, trial_option).astype(jnp.int32)


def draw_element_face_neighbours(key, part):
    positions = jnp.arange(ELEMS, dtype=jnp.int32)
    reach = jax.random.randint(jax.random.fold_in(key, 21), (N_GRP, 6, ELEMS), 1, HE + 1)
    sign = jax.random.randint(jax.random.fold_in(key, 22), (N_GRP, 6, ELEMS), 0, 2) * 2 - 1
    trial_option = positions[None, None, :] + reach * sign
    return jnp.where((trial_option < 0) | (trial_option >= ELEMS), -1, trial_option).astype(jnp.int32)


def draw_tile_target(key, part):
    devices = N_GRP * N_SFC
    serial = jnp.arange(devices, dtype=jnp.int32)
    column = serial % N_SFC
    counts = jax.random.randint(jax.random.fold_in(key, 31), (devices,), FT - CAP, CAP + 1)
    pick = jax.random.randint(jax.random.fold_in(key, 32), (), 0, (N_GRP - 1) * (N_SFC - 1))
    chosen = pick // (N_SFC - 1) * N_SFC + pick % (N_SFC - 1)
    counts = jnp.where(serial == chosen, FT - CAP, counts)
    counts = jnp.where(column == N_SFC - 1, FT, counts)
    positions = jnp.arange(FT, dtype=jnp.int32)
    owner = column[:, None] + (positions[None, :] >= counts[:, None]).astype(jnp.int32)
    local = jax.random.randint(jax.random.fold_in(key, 33), (devices, FT), 0, E_DEV)
    return (owner * E_DEV + local).reshape(N_GRP, TILES).astype(jnp.int32)


def plant(values, stream_key, low, high):
    place = [jax.random.randint(jax.random.fold_in(stream_key, axis), (), 0, length) for axis, length in enumerate(values.shape)]
    widest = values.shape.index(max(values.shape))
    neighbour = place[:widest] + [(place[widest] + 1) % values.shape[widest]] + place[widest + 1:]
    return values.at[tuple(place)].set(low).at[tuple(neighbour)].set(high)


def steps_of(own_key, dims, split, smallest, high):
    level = 1.0
    for axis_at, blocks in split:
        draws = jax.random.uniform(jax.random.fold_in(jax.random.fold_in(own_key, 6), axis_at), (blocks,), jnp.float32, smallest / len(split), high / len(split))
        level = level * jnp.repeat(jnp.exp(draws), dims[axis_at] // blocks).reshape((-1,) + (1,) * (len(dims) - 1 - axis_at))
    return level


def centred(stream_key, dims, scale, bound, shards=(), held_as=jnp.bfloat16):
    level = steps_of(stream_key, dims, shards, -0.22, 0.18) if shards else 1.0
    entries = jax.random.normal(stream_key, dims, jnp.float32) * scale * level
    return jnp.minimum(jnp.maximum(entries, -bound), bound).astype(held_as)


def setup_inputs(seed: int = 0) -> dict:
    splits = jax.random.split(jax.random.key(seed), 10)
    return {
        "flow_fields": centred(splits[0], (N_GRP, 5, TILES, CELLS), 1.0, 6.0, ((0, 4), (2, 32)), jnp.float32),
        "mean_velocity": centred(splits[1], (N_GRP, 3, TILES, CELLS), 0.5, 3.0, ((0, 4), (2, 32)), jnp.float32),
        "cell_eddy_viscosity": jnp.clip(jnp.exp(math.log(0.08) - 2.0794415 * jax.random.uniform(splits[2], (N_GRP, TILES, CELLS), jnp.float32) ** steps_of(splits[2], (N_GRP, TILES, CELLS), ((0, 4), (1, 32)), -0.2, 0.2)), 0.01, 0.08),
        "tile_links": draw_tile_links(jax.random.fold_in(splits[9], 71), 0),
        "tile_target": draw_tile_target(jax.random.fold_in(splits[9], 71), 0),
        "projector": centred(splits[5], (NP, CELLS), CELLS ** -0.5, 0.5, (), jnp.float32),
        "acoustic_state": centred(splits[6], (N_GRP, 4, NP, ELEMS), 1.0, 6.0, ((0, 4), (3, 32)), jnp.float32),
        "element_face_neighbours": draw_element_face_neighbours(jax.random.fold_in(splits[9], 71), 0),
        "face_codes": plant(jax.random.randint(splits[8], (N_GRP, 6, ELEMS), 0, 4), jax.random.fold_in(splits[8], 1), 0, 3).astype(jnp.int32),
    }


ADVECT = 0.1
RELAX = 0.1
PENALTY = 1.5
ACOUSTIC_STEP = 0.08

def derivative_operators():
    points = np.array([-1.0, -1.0 / np.sqrt(5.0), 1.0 / np.sqrt(5.0), 1.0])
    weights = np.array([1.0 / np.prod([points[col] - points[other] for other in range(4) if other != col]) for col in range(4)])
    derivative_matrix = np.zeros((4, 4))
    for line in range(4):
        for col in range(4):
            if line != col:
                derivative_matrix[line, col] = weights[col] / weights[line] / (points[line] - points[col])
        derivative_matrix[line, line] = -derivative_matrix[line].sum()
    identity = np.eye(4)
    return np.stack([np.kron(identity, np.kron(identity, derivative_matrix)), np.kron(identity, np.kron(derivative_matrix, identity)), np.kron(derivative_matrix, np.kron(identity, identity))]).astype(np.float32)

def face_tables():
    faces = []
    for face in range(6):
        axis_id = face // 2
        level = 3 * (face % 2)
        members = []
        for second in range(4):
            for first in range(4):
                coords = [first, second]
                coords.insert(axis_id, level)
                members.append(coords[0] + 4 * coords[1] + 16 * coords[2])
        faces.append(members)
    turns = []
    for turn in range(4):
        mapping = []
        for second in range(4):
            for first in range(4):
                if turn == 0:
                    source = (first, second)
                elif turn == 1:
                    source = (3 - second, first)
                elif turn == 2:
                    source = (3 - first, 3 - second)
                else:
                    source = (second, 3 - first)
                mapping.append(source[0] + 4 * source[1])
        turns.append(mapping)
    return (np.array(faces), np.array(turns))

def flow_advance(solver_state, own_rows, links, viscosity):
    center = jnp.take(solver_state, own_rows, axis=1)
    north = jnp.take(solver_state, links[0], axis=1)
    south = jnp.take(solver_state, links[1], axis=1)
    upper = jnp.take(solver_state, links[2], axis=1)
    lower = jnp.take(solver_state, links[3], axis=1)
    east = jnp.roll(center, -1, axis=2)
    west = jnp.roll(center, 1, axis=2)
    laplace = east + west + north + south + upper + lower - 6.0 * center
    advection = center[1] * (east - west) * 0.5 + center[2] * (north - south) * 0.5 + center[3] * (upper - lower) * 0.5
    return center + viscosity * laplace - ADVECT * advection

def lamb_vector(solver_state, own_rows, links):
    velocity = solver_state[1:4]
    center = jnp.take(velocity, own_rows, axis=1)
    east = jnp.roll(center, -1, axis=2)
    west = jnp.roll(center, 1, axis=2)
    along_x = (east - west) * 0.5
    along_y = (jnp.take(velocity, links[0], axis=1) - jnp.take(velocity, links[1], axis=1)) * 0.5
    along_z = (jnp.take(velocity, links[2], axis=1) - jnp.take(velocity, links[3], axis=1)) * 0.5
    vort_x = along_y[2] - along_z[1]
    vort_y = along_z[0] - along_x[2]
    vort_z = along_x[1] - along_y[0]
    return jnp.stack([vort_y * center[2] - vort_z * center[1], vort_z * center[0] - vort_x * center[2], vort_x * center[1] - vort_y * center[0]])

def project(lamb, average, projector):
    packed = jnp.concatenate([lamb, average], 0)
    mapped = jnp.einsum('ctm,nm->tcn', packed, projector, precision=lax.Precision.HIGHEST)
    return mapped.reshape(mapped.shape[0], -1).astype(jnp.bfloat16)

def acoustic_advance(solver_state, wide, links, valid, codes, source):
    derivative_matrix = jnp.asarray(derivative_operators())
    faces, turns = face_tables()
    gradient_fields = jnp.einsum('yws,lsb->ylwb', derivative_matrix, solver_state, precision=lax.Precision.HIGHEST)
    lamb_src = source[0:3]
    mean_flow = source[3:6]
    convect = mean_flow[0][None] * gradient_fields[0] + mean_flow[1][None] * gradient_fields[1] + mean_flow[2][None] * gradient_fields[2]
    rhs_parts = [-(gradient_fields[0, 1] + gradient_fields[1, 2] + gradient_fields[2, 3]) - convect[0]]
    for direction in range(3):
        rhs_parts.append(-gradient_fields[direction, 0] - convect[1 + direction] - lamb_src[direction])
    rhs = jnp.stack(rhs_parts)
    for face in range(6):
        facing = wide[:, faces[face ^ 1], :]
        remote = jnp.take(facing, links[face], axis=2)
        turned = jnp.zeros_like(remote)
        for turn in range(4):
            turned = turned + jnp.where(codes[face][None, None, :] == turn, remote[:, turns[turn], :], jnp.float32(0.0))
        jump = jnp.where(valid[face][None, None, :], turned - solver_state[:, faces[face], :], jnp.float32(0.0))
        rhs = rhs.at[:, faces[face], :].add(PENALTY * jump)
    return solver_state + ACOUSTIC_STEP * rhs

def gather_sources(rows, ids, count):
    index = jnp.where(ids < 0, count, ids).astype(jnp.int32)
    sums = jnp.zeros((count + 1, rows.shape[1]), jnp.float32).at[index].add(rows.astype(jnp.float32))
    counts = jnp.zeros((count + 1,), jnp.float32).at[index].add(jnp.where(ids < 0, jnp.float32(0.0), jnp.float32(1.0)))
    source = sums[:count] / jnp.maximum(counts[:count], 1.0)[:, None]
    return jnp.transpose(source.reshape(count, 6, -1), (1, 2, 0))

def reference(flow_fields, mean_velocity, cell_eddy_viscosity, tile_links, tile_target, projector, acoustic_state, element_face_neighbours, face_codes):

    def flow_row(solver_state, average, viscosity, neighbours):
        total = solver_state.shape[1]
        own_rows = jnp.arange(total, dtype=jnp.int32)
        links = jnp.where(neighbours < 0, own_rows[None, :], neighbours).astype(jnp.int32)
        payloads = []
        for turn in range(2):
            solver_state = flow_advance(solver_state, own_rows, links, viscosity)
            lamb = lamb_vector(solver_state, own_rows, links)
            average = (1.0 - RELAX) * average + RELAX * solver_state[1:4]
            payloads.append(project(lamb, average, projector))
        return (solver_state, average, jnp.stack(payloads))
    new_fields, new_mean, payloads = jax.vmap(flow_row)(flow_fields, mean_velocity, cell_eddy_viscosity, tile_links)
    flow_rows = N_GRP - 1
    targets = tile_target[:flow_rows].reshape(-1)
    last = N_GRP - 1
    solver_state = acoustic_state[last]
    neighbours = element_face_neighbours[last]
    valid = neighbours >= 0
    links = jnp.where(valid, neighbours, 0).astype(jnp.int32)
    for turn in range(2):
        rows = payloads[:flow_rows, turn].reshape(-1, payloads.shape[-1])
        source = gather_sources(rows, targets, solver_state.shape[2])
        solver_state = acoustic_advance(solver_state, solver_state, links, valid, face_codes[last], source)
    is_flow = (jnp.arange(N_GRP) < flow_rows)[:, None, None, None]
    flow_out = jnp.where(is_flow, new_fields, flow_fields)
    mean_velocity_output = jnp.where(is_flow, new_mean, mean_velocity)
    acoustic_out = acoustic_state.at[last].set(solver_state)
    return (flow_out, mean_velocity_output, acoustic_out)
```

```python
import functools

import jax
import jax.numpy as jnp
import numpy as np
from jax import lax
from jax.experimental import pallas as pl
from jax.experimental.pallas import tpu as pltpu
from jax.sharding import PartitionSpec as P

MESH = pl.DeviceIdType.MESH
F32 = jnp.float32
BF16 = jnp.bfloat16

HW = 16
FT = 256
CELLS = 128
HALO = 3 * HW
WIDE = FT + 2 * HALO
BAND = 160
EL = 256
NP = 64
TURNS = 2


def derivative_operators():
    points = np.array([-1.0, -1.0 / np.sqrt(5.0), 1.0 / np.sqrt(5.0), 1.0])
    weights = np.array(
        [
            1.0 / np.prod([points[col] - points[other] for other in range(4) if other != col])
            for col in range(4)
        ]
    )
    matrix = np.zeros((4, 4))
    for line in range(4):
        for col in range(4):
            if line != col:
                matrix[line, col] = weights[col] / weights[line] / (points[line] - points[col])
        matrix[line, line] = -matrix[line].sum()
    eye = np.eye(4)
    return np.concatenate(
        [
            np.kron(eye, np.kron(eye, matrix)),
            np.kron(eye, np.kron(matrix, eye)),
            np.kron(matrix, np.kron(eye, eye)),
        ]
    ).astype(np.float32)


def face_tables():
    faces = []
    for face in range(6):
        axis, level = face // 2, 3 * (face % 2)
        members = []
        for second in range(4):
            for first in range(4):
                coords = [first, second]
                coords.insert(axis, level)
                members.append(coords[0] + 4 * coords[1] + 16 * coords[2])
        faces.append(members)
    turns = []
    for turn in range(4):
        mapping = []
        for second in range(4):
            for first in range(4):
                source = ((first, second), (3 - second, first), (3 - first, 3 - second), (second, 3 - first))[turn]
                mapping.append(source[0] + 4 * source[1])
        turns.append(mapping)
    return faces, turns


def constants():
    deriv = jnp.asarray(derivative_operators())
    high = deriv.astype(BF16)
    low = (deriv - high.astype(F32)).astype(BF16)
    deriv3 = jnp.concatenate([high, high, low], 1)
    faces, turns = face_tables()
    pick = np.zeros((96, NP), np.float32)
    put = np.zeros((NP, 4 * 96), np.float32)
    for face in range(6):
        for p in range(16):
            pick[16 * face + p, faces[face ^ 1][p]] = 1
            for turn in range(4):
                put[faces[face][p], 96 * turn + 16 * face + turns[turn][p]] = 1
    return deriv3, jnp.asarray(pick, BF16), jnp.asarray(put, BF16)


def halves(x):
    high = x.astype(BF16)
    return high, (x - high.astype(F32)).astype(BF16)


def dot(a, b):
    return lax.dot_general(a, b, (((1,), (0,)), ((), ())), preferred_element_type=F32)


def dot_t(a, b):
    return lax.dot_general(a, b, (((1,), (1,)), ((), ())), preferred_element_type=F32)


def kernel(
    n_sfc,
    ff, mv, cv, tl, tt, pj, ac, en, fc, d3_h, pick_h, put_h,
    fo, mo, ao,
    w0, w1, vis, lk, mean, sel, xb, pay, tgt, oht, pb, res, proj,
    st, sb, hl, hr, enb, fcb, d3, pick, put, ohf, grad, src,
    ls, hs, hrs, ts, trs, ps, prs, rs, rrs, as_, ars, outs,
):
    g = lax.axis_index("grp")
    s = lax.axis_index("sfc")
    right = lax.rem(s + 1, n_sfc)
    left = lax.rem(s + n_sfc - 1, n_sfc)
    first = s * FT
    barrier = pltpu.get_barrier_semaphore()

    def greet(gg, ss):
        pl.semaphore_signal(barrier, inc=1, device_id=(gg, ss), device_id_type=MESH)

    @pl.when(g < 3)
    def _():
        greet(3, s)
        for d in range(3):
            w = lax.rem(g + d, 3)
            if d:
                greet(w, s)
            greet(w, right)
            greet(w, left)

    @pl.when(g == 3)
    def _():
        for w in range(3):
            greet(w, s)
        greet(3, left)
        greet(3, right)

    def load(source, target, k):
        copy = pltpu.make_async_copy(source, target, ls.at[k])
        copy.start()
        return copy

    def remote(source, target, send, recv, gg, ss):
        return pltpu.make_async_remote_copy(
            src_ref=source, dst_ref=target, send_sem=send, recv_sem=recv,
            device_id=(gg, ss), device_id_type=MESH,
        )

    load_state = load(ff, w0.at[:, HALO : HALO + FT, :], 0)
    load_mean = load(mv, mean, 1)
    load_sound = load(ac, st, 2)

    @pl.when(g < 3)
    def _():
        loads = [
            load(cv, vis.at[HALO : HALO + FT, :], 3),
            load(tl, lk.at[0:4, 128 : 128 + FT], 4),
            load(tt, tgt.at[0], 5),
            load(pj, proj, 6),
        ]
        pl.semaphore_wait(barrier, 9)
        halo = []
        for k, (source, target) in enumerate(
            (
                (ff.at[:, 0:HALO, :], w0.at[:, HALO + FT : WIDE, :]),
                (cv.at[0:HALO, :], vis.at[HALO + FT : WIDE, :]),
                (tl.at[:, 0:128], lk.at[0:4, 128 + FT : 256 + FT]),
            )
        ):
            halo.append(remote(source, target, hs.at[k], hrs.at[k], g, left))
        for k, (source, target) in enumerate(
            (
                (ff.at[:, FT - HALO : FT, :], w0.at[:, 0:HALO, :]),
                (cv.at[FT - HALO : FT, :], vis.at[0:HALO, :]),
                (tl.at[:, FT - 128 : FT], lk.at[0:4, 0:128]),
            )
        ):
            halo.append(remote(source, target, hs.at[3 + k], hrs.at[3 + k], g, right))
        for k in (0, 3, 2, 5, 1, 4):
            halo[k].start()
        targets = []
        for d in range(3):
            w = lax.rem(g + d, 3)
            for h, ss in ((0, s), (1, right)):
                if d or h:
                    k = 2 * d + h
                    copy = remote(tt, tgt.at[k], ts.at[k], trs.at[k], w, ss)
                    copy.start()
                    targets.append(copy)
        lk[4:8, :] = jnp.zeros((4, 2 * 128 + FT), jnp.int32)
        for copy in loads:
            copy.wait()
        load_state.wait()
        load_mean.wait()
        for copy in halo:
            copy.wait()

        cols = lax.broadcasted_iota(jnp.int32, (BAND, 256), 1)
        own = lax.broadcasted_iota(jnp.int32, (BAND, 1), 0)
        lt = jnp.transpose(lk[...])
        for b in range(2):
            links = lt[96 + BAND * b : 96 + BAND * (b + 1), :]
            hot = []
            for k in range(4):
                link = links[:, k : k + 1]
                at = jnp.where(
                    link < 0, own + (HW + BAND * b - 96 * b), link - (first - HALO + 96 * b)
                )
                hot.append(jnp.where(cols == at, F32(1.0), F32(0.0)))
            sel[b, 0:BAND, :] = (hot[0] + hot[1] + hot[2] + hot[3]).astype(BF16)
            sel[b, BAND : 2 * BAND, :] = (hot[0] - hot[1]).astype(BF16)
            sel[b, 2 * BAND : 3 * BAND, :] = (hot[2] - hot[3]).astype(BF16)

        ph, plow = halves(proj[...])
        p2 = jnp.concatenate([ph, ph], 1)

        def gather(b, window):
            r = dot(sel[b], jnp.concatenate(halves(window), 1))
            r = r[:, :CELLS] + r[:, CELLS:]
            return r[0:BAND], r[BAND : 2 * BAND], r[2 * BAND :]

        def east_west(c):
            return pltpu.roll(c, CELLS - 1, 1), pltpu.roll(c, 1, 1)

        def advance(source, target, b, fields):
            r0, c0 = HW + BAND * b, 96 * b
            velocity = [source[f, r0 : r0 + BAND, :] for f in (1, 2, 3)]
            nu = vis[r0 : r0 + BAND, :]
            differences = []
            for f in fields:
                c = source[f, r0 : r0 + BAND, :]
                around, d2, d3_ = gather(b, source[f, c0 : c0 + 256, :])
                east, west = east_west(c)
                d1 = east - west
                target[f, r0 : r0 + BAND, :] = (
                    c
                    + nu * (east + west + around - 6.0 * c)
                    - 0.05 * (velocity[0] * d1 + velocity[1] * d2 + velocity[2] * d3_)
                )
                differences.append((d1, d2, d3_))
            return velocity, differences

        def sources(b, velocity, differences, turn):
            (u1, u2, u3), (v1, v2, v3), (w1_, w2_, w3_) = differences
            u, v, w = velocity
            vx = 0.5 * (w2_ - v3)
            vy = 0.5 * (u3 - w1_)
            vz = 0.5 * (v1 - u2)
            packed = [vy * w - vz * v, vz * u - vx * w, vx * v - vy * u]
            rows = slice(128 * b, 128 * b + 128)
            for k in range(3):
                m = 0.9 * mean[k, rows, :] + 0.1 * velocity[k]
                mean[k, rows, :] = m
                packed.append(m)
            for k in range(6):
                hi, lo = halves(packed[k])
                xb[k, rows, 0:128] = hi
                xb[k, rows, 128:256] = lo

        def own_rows(b, x):
            o = 2 * HW if b == 0 else 0
            return x[o : o + 128]

        def send_payload(turn):
            for k in range(6):
                x = xb[k]
                pay[turn, NP * k : NP * (k + 1), :] = (
                    dot_t(p2, x) + dot_t(plow, x[:, 0:128])
                ).astype(BF16)
            copies = []
            for d in (1, 2, 0):
                w = lax.rem(g + d, 3)
                for h, ss in ((0, s), (1, right)):
                    if d or h:
                        k = 2 * d + h
                        copy = remote(
                            pay.at[turn, pl.ds(pl.multiple_of(128 * w, 128), 128), :],
                            pb.at[turn, k], ps.at[turn, k], prs.at[turn, k], w, ss,
                        )
                        copy.start()
                        copies.append(copy)
            return copies

        for b in range(2):
            advance(w0, w1, b, (0, 1, 2, 3, 4))
        w1[:, 0:HW, :] = w0[:, 0:HW, :]
        w1[:, WIDE - HW : WIDE, :] = w0[:, WIDE - HW : WIDE, :]
        for b in range(2):
            velocity, differences = advance(w1, w0, b, (1, 2, 3))
            sources(
                b,
                [own_rows(b, x) for x in velocity],
                [[own_rows(b, x) for x in d] for d in differences],
                0,
            )
        payloads = [send_payload(0)]
        for b in range(2):
            o = HALO + 128 * b
            c0 = 96 * b
            velocity, differences = [], []
            i0 = 2 * HW if b == 0 else 0
            rows = jnp.concatenate(
                [
                    sel[b, BAND + i0 : BAND + i0 + 128, :],
                    sel[b, 2 * BAND + i0 : 2 * BAND + i0 + 128, :],
                ],
                0,
            )
            for f in (1, 2, 3):
                c = w0[f, o : o + 128, :]
                r = dot(rows, jnp.concatenate(halves(w0[f, c0 : c0 + 256, :]), 1))
                r = r[:, :CELLS] + r[:, CELLS:]
                east, west = east_west(c)
                velocity.append(c)
                differences.append((east - west, r[0:128], r[128:256]))
            sources(b, velocity, differences, 1)
        payloads.append(send_payload(1))
        for b in range(2):
            advance(w1, w0, b, (0, 4))

        for copy in targets:
            copy.wait()
        element = lax.broadcasted_iota(jnp.int32, (EL, FT), 0) + s * EL
        count = jnp.zeros((16, EL), F32)
        ones = jnp.ones((16, FT), BF16)
        for k in range(6):
            hot = jnp.where(tgt[k] == element, F32(1.0), F32(0.0)).astype(BF16)
            oht[k] = hot
            count = count + dot_t(ones, hot)
        inverse = 1.0 / jnp.maximum(count[0:1], 1.0)
        results = []
        mine = pl.ds(pl.multiple_of(128 * g, 128), 128)
        for turn in range(TURNS):
            total = dot_t(pay[turn, mine, :], oht[0])
            for copy in payloads[turn]:
                copy.wait()
            for k in range(1, 6):
                total = total + dot_t(pb[turn, k], oht[k])
            res[turn] = (total * inverse).astype(BF16)
            copy = remote(res.at[turn], src.at[turn, mine, :], rs.at[turn], rrs.at[turn, g], 3, s)
            copy.start()
            results.append(copy)
        load_sound.wait()
        writes = [
            pltpu.make_async_copy(w0.at[:, HALO : HALO + FT, :], fo, outs.at[0]),
            pltpu.make_async_copy(mean, mo, outs.at[1]),
            pltpu.make_async_copy(st, ao, outs.at[2]),
        ]
        for copy in writes:
            copy.start()
        for copy in results:
            copy.wait_send()
        for copy in writes:
            copy.wait()

    @pl.when(g == 3)
    def _():
        loads = [
            load(en, enb, 3),
            load(fc, fcb, 4),
            load(d3_h, d3, 5),
            load(pick_h, pick, 6),
            load(put_h, put, 7),
        ]
        pl.semaphore_wait(barrier, 5)
        load_sound.wait()

        def send_state(turn):
            for v in range(4):
                sb[turn, NP * v : NP * (v + 1), :] = st[v].astype(BF16)
            copies = [
                remote(sb.at[turn, :, 0:128], hr.at[turn], as_.at[turn, 0], ars.at[turn, 0], 3, left),
                remote(sb.at[turn, :, 128:256], hl.at[turn], as_.at[turn, 1], ars.at[turn, 1], 3, right),
            ]
            for copy in copies:
                copy.start()
            return copies

        sends = send_state(0)
        load_state.wait()
        load_mean.wait()
        writes = [
            pltpu.make_async_copy(w0.at[:, HALO : HALO + FT, :], fo, outs.at[0]),
            pltpu.make_async_copy(mean, mo, outs.at[1]),
        ]
        for copy in writes:
            copy.start()
        for copy in loads:
            copy.wait()

        row = lax.broadcasted_iota(jnp.int32, (EL + 128, EL), 0)
        for f in range(6):
            link = enb[f : f + 1, :]
            at = link - s * EL
            at = jnp.where(link < 0, 999, jnp.where(at < 0, at + (EL + 128), at))
            ohf[f] = jnp.where(row == at, F32(1.0), F32(0.0)).astype(BF16)
        node = lax.broadcasted_iota(jnp.int32, (NP, EL), 0)
        faces_on = jnp.zeros((NP, EL), F32)
        for f in range(6):
            coordinate = (node >> (2 * (f // 2))) & 3
            valid = jnp.where(enb[f : f + 1, :] >= 0, F32(1.0), F32(0.0))
            faces_on = faces_on + jnp.where(coordinate == 3 * (f % 2), valid, F32(0.0))
        lane = lax.broadcasted_iota(jnp.int32, (4 * NP, 128), 1)

        for turn in range(TURNS):
            for v in range(4):
                hi, lo = halves(st[v])
                grad[v] = dot(d3[...], jnp.concatenate([hi, lo, hi], 0))
            for copy in sends:
                copy.wait()
            ends = jnp.where(lane < HW, hr[turn].astype(F32), hl[turn].astype(F32)).astype(BF16)
            facing = []
            for v in range(4):
                rows = slice(NP * v, NP * (v + 1))
                wide = jnp.concatenate([sb[turn, rows, :], ends[rows]], 1)
                facing.append(dot(pick[...], wide).astype(BF16))
            remotes = []
            for f in range(6):
                stacked = jnp.concatenate([facing[v][16 * f : 16 * f + 16] for v in range(4)], 0)
                remotes.append(dot(stacked, ohf[f]))
            before = []
            for v in range(4):
                turned = []
                for r in range(4):
                    for f in range(6):
                        turned.append(
                            jnp.where(
                                fcb[f : f + 1, :] == r, remotes[f][16 * v : 16 * v + 16], F32(0.0)
                            ).astype(BF16)
                        )
                jump = dot(put[...], jnp.concatenate(turned, 0)) - faces_on * st[v]
                if v == 0:
                    linear = grad[1, 0:64] + grad[2, 64:128] + grad[3, 128:192]
                else:
                    linear = grad[0, 64 * (v - 1) : 64 * v]
                before.append(st[v] + 0.08 * (1.5 * jump - linear))
            for w in range(3):
                rows = slice(128 * w, 128 * w + 128)
                remote(
                    res.at[turn], src.at[turn, rows, :], rs.at[turn], rrs.at[turn, w], w, s
                ).wait_recv()
            flow = [src[turn, 192 + 64 * d : 256 + 64 * d, :].astype(F32) for d in range(3)]
            for v in range(4):
                convect = sum(flow[d] * grad[v, 64 * d : 64 * d + 64] for d in range(3))
                if v:
                    convect = convect + src[turn, 64 * (v - 1) : 64 * v, :].astype(F32)
                st[v] = before[v] - 0.08 * convect
            if turn == 0:
                sends = send_state(1)
        write = pltpu.make_async_copy(st, ao, outs.at[2])
        write.start()
        for copy in writes:
            copy.wait()
        write.wait()


def body(ff, mv, cv, tl, tt, pj, ac, en, fc):
    n_sfc = lax.axis_size("sfc")
    any_space = pl.BlockSpec(memory_space=pl.ANY)
    dma = pltpu.SemaphoreType.DMA
    outs = pl.pallas_call(
        functools.partial(kernel, n_sfc),
        out_shape=(
            jax.ShapeDtypeStruct((5, FT, CELLS), F32),
            jax.ShapeDtypeStruct((3, FT, CELLS), F32),
            jax.ShapeDtypeStruct((4, NP, EL), F32),
        ),
        in_specs=[any_space] * 12,
        out_specs=(any_space,) * 3,
        scratch_shapes=[
            pltpu.VMEM((5, WIDE, CELLS), F32),
            pltpu.VMEM((5, WIDE, CELLS), F32),
            pltpu.VMEM((WIDE, CELLS), F32),
            pltpu.VMEM((8, 256 + FT), jnp.int32),
            pltpu.VMEM((3, FT, CELLS), F32),
            pltpu.VMEM((2, 3 * BAND, 256), BF16),
            pltpu.VMEM((6, FT, 256), BF16),
            pltpu.VMEM((TURNS, 6 * NP, FT), BF16),
            pltpu.VMEM((6, 1, FT), jnp.int32),
            pltpu.VMEM((6, EL, FT), BF16),
            pltpu.VMEM((TURNS, 6, 128, FT), BF16),
            pltpu.VMEM((TURNS, 128, EL), BF16),
            pltpu.VMEM((NP, CELLS), F32),
            pltpu.VMEM((4, NP, EL), F32),
            pltpu.VMEM((TURNS, 4 * NP, EL), BF16),
            pltpu.VMEM((TURNS, 4 * NP, 128), BF16),
            pltpu.VMEM((TURNS, 4 * NP, 128), BF16),
            pltpu.VMEM((6, EL), jnp.int32),
            pltpu.VMEM((6, EL), jnp.int32),
            pltpu.VMEM((192, 192), BF16),
            pltpu.VMEM((96, NP), BF16),
            pltpu.VMEM((NP, 384), BF16),
            pltpu.VMEM((6, EL + 128, EL), BF16),
            pltpu.VMEM((4, 192, EL), F32),
            pltpu.VMEM((TURNS, 6 * NP, EL), BF16),
            dma((8,)),
            dma((6,)), dma((6,)),
            dma((6,)), dma((6,)),
            dma((TURNS, 6)), dma((TURNS, 6)),
            dma((TURNS,)), dma((TURNS, 3)),
            dma((TURNS, 2)), dma((TURNS, 2)),
            dma((3,)),
        ],
        compiler_params=pltpu.CompilerParams(
            collective_id=0, has_side_effects=True, vmem_limit_bytes=48 * 1024 * 1024
        ),
    )(ff[0], mv[0], cv[0], tl[0], tt, pj, ac[0], en[0], fc[0], *constants())
    return tuple(o[None] for o in outs)


def solution(mesh):
    placed = (
        P("grp", None, "sfc", None),
        P("grp", None, "sfc", None),
        P("grp", "sfc", None),
        P("grp", None, "sfc"),
        P("grp", "sfc"),
        P(),
        P("grp", None, None, "sfc"),
        P("grp", None, "sfc"),
        P("grp", None, "sfc"),
    )
    return jax.shard_map(
        body,
        mesh=mesh,
        in_specs=placed,
        out_specs=(
            P("grp", None, "sfc", None),
            P("grp", None, "sfc", None),
            P("grp", None, None, "sfc"),
        ),
        check_vma=False,
    )
```

```python
import functools

import jax
import jax.numpy as jnp
import numpy as np
from jax import lax
from jax.experimental import pallas as pl
from jax.experimental.pallas import tpu as pltpu
from jax.sharding import PartitionSpec as P

MESH = pl.DeviceIdType.MESH
F32 = jnp.float32
BF16 = jnp.bfloat16

HW = 16
FT = 256
CELLS = 128
HALO = 3 * HW
WIDE = FT + 2 * HALO
BAND = 160
EL = 256
NP = 64
TURNS = 2


def derivative_operators():
    points = np.array([-1.0, -1.0 / np.sqrt(5.0), 1.0 / np.sqrt(5.0), 1.0])
    weights = np.array(
        [
            1.0 / np.prod([points[col] - points[other] for other in range(4) if other != col])
            for col in range(4)
        ]
    )
    matrix = np.zeros((4, 4))
    for line in range(4):
        for col in range(4):
            if line != col:
                matrix[line, col] = weights[col] / weights[line] / (points[line] - points[col])
        matrix[line, line] = -matrix[line].sum()
    eye = np.eye(4)
    return np.concatenate(
        [
            np.kron(eye, np.kron(eye, matrix)),
            np.kron(eye, np.kron(matrix, eye)),
            np.kron(matrix, np.kron(eye, eye)),
        ]
    ).astype(np.float32)


def face_tables():
    faces = []
    for face in range(6):
        axis, level = face // 2, 3 * (face % 2)
        members = []
        for second in range(4):
            for first in range(4):
                coords = [first, second]
                coords.insert(axis, level)
                members.append(coords[0] + 4 * coords[1] + 16 * coords[2])
        faces.append(members)
    turns = []
    for turn in range(4):
        mapping = []
        for second in range(4):
            for first in range(4):
                source = ((first, second), (3 - second, first), (3 - first, 3 - second), (second, 3 - first))[turn]
                mapping.append(source[0] + 4 * source[1])
        turns.append(mapping)
    return faces, turns


def constants():
    deriv = jnp.asarray(derivative_operators())
    high = deriv.astype(BF16)
    low = (deriv - high.astype(F32)).astype(BF16)
    deriv3 = jnp.concatenate([high, high, low], 1)
    faces, turns = face_tables()
    pick = np.zeros((96, NP), np.float32)
    put = np.zeros((NP, 4 * 96), np.float32)
    for face in range(6):
        for p in range(16):
            pick[16 * face + p, faces[face ^ 1][p]] = 1
            for turn in range(4):
                put[faces[face][p], 96 * turn + 16 * face + turns[turn][p]] = 1
    return deriv3, jnp.asarray(pick, BF16), jnp.asarray(put, BF16)


def halves(x):
    high = x.astype(BF16)
    return high, (x - high.astype(F32)).astype(BF16)


def dot(a, b):
    return lax.dot_general(a, b, (((1,), (0,)), ((), ())), preferred_element_type=F32)


def dot_t(a, b):
    return lax.dot_general(a, b, (((1,), (1,)), ((), ())), preferred_element_type=F32)


def kernel(
    n_sfc,
    ff, mv, cv, tl, tt, pj, ac, en, fc, d3_h, pick_h, put_h,
    fo, mo, ao,
    w0, w1, vis, lk, mean, sel, xb, pay, tgt, oht, pb, res, proj,
    st, sb, hl, hr, enb, fcb, d3, pick, put, ohf, grad, src,
    ls, hs, hrs, ts, trs, ps, prs, rs, rrs, as_, ars, outs,
):
    g = lax.axis_index("grp")
    s = lax.axis_index("sfc")
    right = lax.rem(s + 1, n_sfc)
    left = lax.rem(s + n_sfc - 1, n_sfc)
    first = s * FT
    barrier = pltpu.get_barrier_semaphore()

    def greet(gg, ss):
        pl.semaphore_signal(barrier, inc=1, device_id=(gg, ss), device_id_type=MESH)

    @pl.when(g < 3)
    def _():
        greet(3, s)
        for d in range(3):
            w = lax.rem(g + d, 3)
            if d:
                greet(w, s)
            greet(w, right)
            greet(w, left)

    @pl.when(g == 3)
    def _():
        for w in range(3):
            greet(w, s)
        greet(3, left)
        greet(3, right)

    def load(source, target, k):
        copy = pltpu.make_async_copy(source, target, ls.at[k])
        copy.start()
        return copy

    def remote(source, target, send, recv, gg, ss):
        return pltpu.make_async_remote_copy(
            src_ref=source, dst_ref=target, send_sem=send, recv_sem=recv,
            device_id=(gg, ss), device_id_type=MESH,
        )

    load_state = load(ff, w0.at[:, HALO : HALO + FT, :], 0)
    load_mean = load(mv, mean, 1)
    load_sound = load(ac, st, 2)

    @pl.when(g < 3)
    def _():
        loads = [
            load(cv, vis.at[HALO : HALO + FT, :], 3),
            load(tl, lk.at[0:4, 128 : 128 + FT], 4),
            load(tt, tgt.at[0], 5),
            load(pj, proj, 6),
        ]
        pl.semaphore_wait(barrier, 9)
        halo = []
        for k, (source, target) in enumerate(
            (
                (ff.at[:, 0:HALO, :], w0.at[:, HALO + FT : WIDE, :]),
                (cv.at[0:HALO, :], vis.at[HALO + FT : WIDE, :]),
                (tl.at[:, 0:128], lk.at[0:4, 128 + FT : 256 + FT]),
            )
        ):
            halo.append(remote(source, target, hs.at[k], hrs.at[k], g, left))
        for k, (source, target) in enumerate(
            (
                (ff.at[:, FT - HALO : FT, :], w0.at[:, 0:HALO, :]),
                (cv.at[FT - HALO : FT, :], vis.at[0:HALO, :]),
                (tl.at[:, FT - 128 : FT], lk.at[0:4, 0:128]),
            )
        ):
            halo.append(remote(source, target, hs.at[3 + k], hrs.at[3 + k], g, right))
        for k in (0, 3, 2, 5, 1, 4):
            halo[k].start()
        targets = []
        for d in range(3):
            w = lax.rem(g + d, 3)
            for h, ss in ((0, s), (1, right)):
                if d or h:
                    k = 2 * d + h
                    copy = remote(tt, tgt.at[k], ts.at[k], trs.at[k], w, ss)
                    copy.start()
                    targets.append(copy)
        lk[4:8, :] = jnp.zeros((4, 2 * 128 + FT), jnp.int32)
        for copy in loads:
            copy.wait()
        load_state.wait()
        load_mean.wait()
        for copy in halo:
            copy.wait()

        cols = lax.broadcasted_iota(jnp.int32, (BAND, 256), 1)
        own = lax.broadcasted_iota(jnp.int32, (BAND, 1), 0)
        lt = jnp.transpose(lk[...])
        for b in range(2):
            links = lt[96 + BAND * b : 96 + BAND * (b + 1), :]
            hot = []
            for k in range(4):
                link = links[:, k : k + 1]
                at = jnp.where(
                    link < 0, own + (HW + BAND * b - 96 * b), link - (first - HALO + 96 * b)
                )
                hot.append(jnp.where(cols == at, F32(1.0), F32(0.0)))
            sel[b, 0:BAND, :] = (hot[0] + hot[1] + hot[2] + hot[3]).astype(BF16)
            sel[b, BAND : 2 * BAND, :] = (hot[0] - hot[1]).astype(BF16)
            sel[b, 2 * BAND : 3 * BAND, :] = (hot[2] - hot[3]).astype(BF16)

        ph, plow = halves(proj[...])
        p2 = jnp.concatenate([ph, ph], 1)

        def gather(b, window):
            r = dot(sel[b], jnp.concatenate(halves(window), 1))
            r = r[:, :CELLS] + r[:, CELLS:]
            return r[0:BAND], r[BAND : 2 * BAND], r[2 * BAND :]

        def east_west(c):
            return pltpu.roll(c, CELLS - 1, 1), pltpu.roll(c, 1, 1)

        def advance(source, target, b, fields):
            r0, c0 = HW + BAND * b, 96 * b
            velocity = [source[f, r0 : r0 + BAND, :] for f in (1, 2, 3)]
            nu = vis[r0 : r0 + BAND, :]
            differences = []
            for f in fields:
                c = source[f, r0 : r0 + BAND, :]
                around, d2, d3_ = gather(b, source[f, c0 : c0 + 256, :])
                east, west = east_west(c)
                d1 = east - west
                target[f, r0 : r0 + BAND, :] = (
                    c
                    + nu * (east + west + around - 6.0 * c)
                    - 0.05 * (velocity[0] * d1 + velocity[1] * d2 + velocity[2] * d3_)
                )
                differences.append((d1, d2, d3_))
            return velocity, differences

        def sources(b, velocity, differences, turn):
            (u1, u2, u3), (v1, v2, v3), (w1_, w2_, w3_) = differences
            u, v, w = velocity
            vx = 0.5 * (w2_ - v3)
            vy = 0.5 * (u3 - w1_)
            vz = 0.5 * (v1 - u2)
            packed = [vy * w - vz * v, vz * u - vx * w, vx * v - vy * u]
            rows = slice(128 * b, 128 * b + 128)
            for k in range(3):
                m = 0.9 * mean[k, rows, :] + 0.1 * velocity[k]
                mean[k, rows, :] = m
                packed.append(m)
            for k in range(6):
                hi, lo = halves(packed[k])
                xb[k, rows, 0:128] = hi
                xb[k, rows, 128:256] = lo

        def own_rows(b, x):
            o = 2 * HW if b == 0 else 0
            return x[o : o + 128]

        def send_payload(turn):
            for k in range(6):
                x = xb[k]
                pay[turn, NP * k : NP * (k + 1), :] = (
                    dot_t(p2, x) + dot_t(plow, x[:, 0:128])
                ).astype(BF16)
            copies = []
            for d in (1, 2, 0):
                w = lax.rem(g + d, 3)
                for h, ss in ((0, s), (1, right)):
                    if d or h:
                        k = 2 * d + h
                        copy = remote(
                            pay.at[turn, pl.ds(pl.multiple_of(128 * w, 128), 128), :],
                            pb.at[turn, k], ps.at[turn, k], prs.at[turn, k], w, ss,
                        )
                        copy.start()
                        copies.append(copy)
            return copies

        for b in range(2):
            advance(w0, w1, b, (0, 1, 2, 3, 4))
        w1[:, 0:HW, :] = w0[:, 0:HW, :]
        w1[:, WIDE - HW : WIDE, :] = w0[:, WIDE - HW : WIDE, :]
        for b in range(2):
            velocity, differences = advance(w1, w0, b, (1, 2, 3))
            sources(
                b,
                [own_rows(b, x) for x in velocity],
                [[own_rows(b, x) for x in d] for d in differences],
                0,
            )
        payloads = [send_payload(0)]
        for b in range(2):
            o = HALO + 128 * b
            c0 = 96 * b
            velocity, differences = [], []
            i0 = 2 * HW if b == 0 else 0
            rows = jnp.concatenate(
                [
                    sel[b, BAND + i0 : BAND + i0 + 128, :],
                    sel[b, 2 * BAND + i0 : 2 * BAND + i0 + 128, :],
                ],
                0,
            )
            for f in (1, 2, 3):
                c = w0[f, o : o + 128, :]
                r = dot(rows, jnp.concatenate(halves(w0[f, c0 : c0 + 256, :]), 1))
                r = r[:, :CELLS] + r[:, CELLS:]
                east, west = east_west(c)
                velocity.append(c)
                differences.append((east - west, r[0:128], r[128:256]))
            sources(b, velocity, differences, 1)
        payloads.append(send_payload(1))
        for b in range(2):
            advance(w1, w0, b, (0, 4))

        for copy in targets:
            copy.wait()
        element = lax.broadcasted_iota(jnp.int32, (EL, FT), 0) + s * EL
        count = jnp.zeros((16, EL), F32)
        ones = jnp.ones((16, FT), BF16)
        for k in range(6):
            hot = jnp.where(tgt[k] == element, F32(1.0), F32(0.0)).astype(BF16)
            oht[k] = hot
            count = count + dot_t(ones, hot)
        inverse = 1.0 / jnp.maximum(count[0:1], 1.0)
        results = []
        mine = pl.ds(pl.multiple_of(128 * g, 128), 128)
        for turn in range(TURNS):
            total = dot_t(pay[turn, mine, :], oht[0])
            for copy in payloads[turn]:
                copy.wait()
            for k in range(1, 6):
                total = total + dot_t(pb[turn, k], oht[k])
            res[turn] = (total * inverse).astype(BF16)
            copy = remote(res.at[turn], src.at[turn, mine, :], rs.at[turn], rrs.at[turn, g], 3, s)
            copy.start()
            results.append(copy)
        load_sound.wait()
        writes = [
            pltpu.make_async_copy(w0.at[:, HALO : HALO + FT, :], fo, outs.at[0]),
            pltpu.make_async_copy(mean, mo, outs.at[1]),
            pltpu.make_async_copy(st, ao, outs.at[2]),
        ]
        for copy in writes:
            copy.start()
        for copy in results:
            copy.wait_send()
        for copy in writes:
            copy.wait()

    @pl.when(g == 3)
    def _():
        loads = [
            load(en, enb, 3),
            load(fc, fcb, 4),
            load(d3_h, d3, 5),
            load(pick_h, pick, 6),
            load(put_h, put, 7),
        ]
        pl.semaphore_wait(barrier, 5)
        load_sound.wait()

        def send_state(turn):
            for v in range(4):
                sb[turn, NP * v : NP * (v + 1), :] = st[v].astype(BF16)
            copies = [
                remote(sb.at[turn, :, 0:128], hr.at[turn], as_.at[turn, 0], ars.at[turn, 0], 3, left),
                remote(sb.at[turn, :, 128:256], hl.at[turn], as_.at[turn, 1], ars.at[turn, 1], 3, right),
            ]
            for copy in copies:
                copy.start()
            return copies

        sends = send_state(0)
        load_state.wait()
        load_mean.wait()
        writes = [
            pltpu.make_async_copy(w0.at[:, HALO : HALO + FT, :], fo, outs.at[0]),
            pltpu.make_async_copy(mean, mo, outs.at[1]),
        ]
        for copy in writes:
            copy.start()
        for copy in loads:
            copy.wait()

        row = lax.broadcasted_iota(jnp.int32, (EL + 128, EL), 0)
        for f in range(6):
            link = enb[f]
            at = link - s * EL
            at = jnp.where(link < 0, 999, jnp.where(at < 0, at + (EL + 128), at))
            ohf[f] = jnp.where(row == at, F32(1.0), F32(0.0)).astype(BF16)
        node = lax.broadcasted_iota(jnp.int32, (NP, EL), 0)
        faces_on = jnp.zeros((NP, EL), F32)
        for f in range(6):
            coordinate = (node >> (2 * (f // 2))) & 3
            valid = jnp.where(enb[f] >= 0, F32(1.0), F32(0.0))
            faces_on = faces_on + jnp.where(coordinate == 3 * (f % 2), valid, F32(0.0))
        lane = lax.broadcasted_iota(jnp.int32, (4 * NP, 128), 1)

        for turn in range(TURNS):
            for v in range(4):
                hi, lo = halves(st[v])
                grad[v] = dot(d3[...], jnp.concatenate([hi, lo, hi], 0))
            for copy in sends:
                copy.wait()
            ends = jnp.where(lane < HW, hr[turn].astype(F32), hl[turn].astype(F32)).astype(BF16)
            facing = []
            for v in range(4):
                rows = slice(NP * v, NP * (v + 1))
                wide = jnp.concatenate([sb[turn, rows, :], ends[rows]], 1)
                facing.append(dot(pick[...], wide).astype(BF16))
            remotes = []
            for f in range(6):
                stacked = jnp.concatenate([facing[v][16 * f : 16 * f + 16] for v in range(4)], 0)
                remotes.append(dot(stacked, ohf[f]))
            before = []
            for v in range(4):
                turned = []
                for r in range(4):
                    for f in range(6):
                        turned.append(
                            jnp.where(
                                fcb[f] == r, remotes[f][16 * v : 16 * v + 16], F32(0.0)
                            ).astype(BF16)
                        )
                jump = dot(put[...], jnp.concatenate(turned, 0)) - faces_on * st[v]
                if v == 0:
                    linear = grad[1, 0:64] + grad[2, 64:128] + grad[3, 128:192]
                else:
                    linear = grad[0, 64 * (v - 1) : 64 * v]
                before.append(st[v] + 0.08 * (1.5 * jump - linear))
            for w in range(3):
                rows = slice(128 * w, 128 * w + 128)
                remote(
                    res.at[turn], src.at[turn, rows, :], rs.at[turn], rrs.at[turn, w], w, s
                ).wait_recv()
            flow = [src[turn, 192 + 64 * d : 256 + 64 * d, :].astype(F32) for d in range(3)]
            for v in range(4):
                convect = sum(flow[d] * grad[v, 64 * d : 64 * d + 64] for d in range(3))
                if v:
                    convect = convect + src[turn, 64 * (v - 1) : 64 * v, :].astype(F32)
                st[v] = before[v] - 0.08 * convect
            if turn == 0:
                sends = send_state(1)
        write = pltpu.make_async_copy(st, ao, outs.at[2])
        write.start()
        for copy in writes:
            copy.wait()
        write.wait()


def store(a, b, c, x, y, z, sems):
    copies = [
        pltpu.make_async_copy(source, target, sems.at[k])
        for k, (source, target) in enumerate(((a, x), (b, y), (c, z)))
    ]
    for copy in copies:
        copy.start()
    for copy in copies:
        copy.wait()


def body(ff, mv, cv, tl, tt, pj, ac, en, fc):
    n_sfc = lax.axis_size("sfc")
    hbm = pl.BlockSpec(memory_space=pltpu.MemorySpace.HBM)
    any_space = pl.BlockSpec(memory_space=pl.ANY)
    dma = pltpu.SemaphoreType.DMA
    outs = pl.pallas_call(
        functools.partial(kernel, n_sfc),
        out_shape=(
            jax.ShapeDtypeStruct((5, FT, CELLS), F32),
            jax.ShapeDtypeStruct((3, FT, CELLS), F32),
            jax.ShapeDtypeStruct((4, NP, EL), F32),
        ),
        in_specs=[hbm] * 12,
        out_specs=(any_space,) * 3,
        scratch_shapes=[
            pltpu.VMEM((5, WIDE, CELLS), F32),
            pltpu.VMEM((5, WIDE, CELLS), F32),
            pltpu.VMEM((WIDE, CELLS), F32),
            pltpu.VMEM((8, 256 + FT), jnp.int32),
            pltpu.VMEM((3, FT, CELLS), F32),
            pltpu.VMEM((2, 3 * BAND, 256), BF16),
            pltpu.VMEM((6, FT, 256), BF16),
            pltpu.VMEM((TURNS, 6 * NP, FT), BF16),
            pltpu.VMEM((6, 1, FT), jnp.int32),
            pltpu.VMEM((6, EL, FT), BF16),
            pltpu.VMEM((TURNS, 6, 128, FT), BF16),
            pltpu.VMEM((TURNS, 128, EL), BF16),
            pltpu.VMEM((NP, CELLS), F32),
            pltpu.VMEM((4, NP, EL), F32),
            pltpu.VMEM((TURNS, 4 * NP, EL), BF16),
            pltpu.VMEM((TURNS, 4 * NP, 128), BF16),
            pltpu.VMEM((TURNS, 4 * NP, 128), BF16),
            pltpu.VMEM((6, 1, EL), jnp.int32),
            pltpu.VMEM((6, 1, EL), jnp.int32),
            pltpu.VMEM((192, 192), BF16),
            pltpu.VMEM((96, NP), BF16),
            pltpu.VMEM((NP, 384), BF16),
            pltpu.VMEM((6, EL + 128, EL), BF16),
            pltpu.VMEM((4, 192, EL), F32),
            pltpu.VMEM((TURNS, 6 * NP, EL), BF16),
            dma((8,)),
            dma((6,)), dma((6,)),
            dma((6,)), dma((6,)),
            dma((TURNS, 6)), dma((TURNS, 6)),
            dma((TURNS,)), dma((TURNS, 3)),
            dma((TURNS, 2)), dma((TURNS, 2)),
            dma((3,)),
        ],
        compiler_params=pltpu.CompilerParams(
            collective_id=0, has_side_effects=True, vmem_limit_bytes=48 * 1024 * 1024
        ),
    )(*(
        pltpu.with_memory_space_constraint(x, pltpu.MemorySpace.HBM)
        for x in (
            ff[0], mv[0], cv[0], tl[0], tt, pj, ac[0],
            jnp.swapaxes(en, 0, 1), jnp.swapaxes(fc, 0, 1), *constants(),
        )
    ))
    outs = pl.pallas_call(
        store,
        out_shape=tuple(jax.ShapeDtypeStruct(o.shape, o.dtype) for o in outs),
        in_specs=[any_space] * 3,
        out_specs=(hbm,) * 3,
        scratch_shapes=[dma((3,))],
        compiler_params=pltpu.CompilerParams(vmem_limit_bytes=1024 * 1024),
    )(*outs)
    return tuple(o[None] for o in outs)


def solution(mesh):
    placed = (
        P("grp", None, "sfc", None),
        P("grp", None, "sfc", None),
        P("grp", "sfc", None),
        P("grp", None, "sfc"),
        P("grp", "sfc"),
        P(),
        P("grp", None, None, "sfc"),
        P("grp", None, "sfc"),
        P("grp", None, "sfc"),
    )
    return jax.shard_map(
        body,
        mesh=mesh,
        in_specs=placed,
        out_specs=(
            P("grp", None, "sfc", None),
            P("grp", None, "sfc", None),
            P("grp", None, None, "sfc"),
        ),
        check_vma=False,
    )
```

```python
import functools

import jax
import jax.numpy as jnp
import numpy as np
from jax import lax
from jax.experimental import pallas as pl
from jax.experimental.pallas import tpu as pltpu
from jax.sharding import PartitionSpec as P

MESH = pl.DeviceIdType.MESH
F32 = jnp.float32
BF16 = jnp.bfloat16

HW = 16
FT = 256
CELLS = 128
HALO = 3 * HW
WIDE = FT + 2 * HALO
EL = 256
NP = 64
TURNS = 2
SHARE = 128
ROUTE = {(0, 1): "direct", (0, 0): "direct", (1, 1): "direct", (1, 0): "direct"}


def derivative_operators():
    points = np.array([-1.0, -1.0 / np.sqrt(5.0), 1.0 / np.sqrt(5.0), 1.0])
    weights = np.array(
        [
            1.0 / np.prod([points[col] - points[other] for other in range(4) if other != col])
            for col in range(4)
        ]
    )
    matrix = np.zeros((4, 4))
    for line in range(4):
        for col in range(4):
            if line != col:
                matrix[line, col] = weights[col] / weights[line] / (points[line] - points[col])
        matrix[line, line] = -matrix[line].sum()
    eye = np.eye(4)
    return np.concatenate(
        [
            np.kron(eye, np.kron(eye, matrix)),
            np.kron(eye, np.kron(matrix, eye)),
            np.kron(matrix, np.kron(eye, eye)),
        ]
    ).astype(np.float32)


def face_tables():
    faces = []
    for face in range(6):
        axis, level = face // 2, 3 * (face % 2)
        members = []
        for second in range(4):
            for first in range(4):
                coords = [first, second]
                coords.insert(axis, level)
                members.append(coords[0] + 4 * coords[1] + 16 * coords[2])
        faces.append(members)
    turns = []
    for turn in range(4):
        mapping = []
        for second in range(4):
            for first in range(4):
                source = ((first, second), (3 - second, first), (3 - first, 3 - second), (second, 3 - first))[turn]
                mapping.append(source[0] + 4 * source[1])
        turns.append(mapping)
    return faces, turns


def constants():
    deriv = jnp.asarray(derivative_operators())
    high = deriv.astype(BF16)
    low = (deriv - high.astype(F32)).astype(BF16)
    deriv3 = jnp.concatenate([high, high, low], 1)
    faces, turns = face_tables()
    pick = np.zeros((96, NP), np.float32)
    put = np.zeros((NP, 4 * 96), np.float32)
    for face in range(6):
        for p in range(16):
            pick[16 * face + p, faces[face ^ 1][p]] = 1
            for turn in range(4):
                put[faces[face][p], 96 * turn + 16 * face + turns[turn][p]] = 1
    return deriv3, jnp.asarray(pick, BF16), jnp.asarray(put, BF16)


def halves(x):
    high = x.astype(BF16)
    return high, (x - high.astype(F32)).astype(BF16)


def dot(a, b):
    return lax.dot_general(a, b, (((1,), (0,)), ((), ())), preferred_element_type=F32)


def dot_t(a, b):
    return lax.dot_general(a, b, (((1,), (1,)), ((), ())), preferred_element_type=F32)


def kernel(
    n_sfc,
    ff, mv, cv, tl, tt, pj, ac, en, fc, d3_h, pick_h, put_h,
    fo, mo, ao,
    w0, w1, vis, hb, hn, lk, mean, sel_mid, sel_end, xb, pay, tgt, oht, ohn, pb, away, came, tot, res, proj,
    st, sb, ends, hl, hr, enb, fcb, d3, pick, put, ohf, grad, src,
    ls, hs, hrs, ts, trs, ps, prs, ns, nrs, rs, rrs, as_, ars, outs,
):
    g = lax.axis_index("grp")
    s = lax.axis_index("sfc")
    right = lax.rem(s + 1, n_sfc)
    left = lax.rem(s + n_sfc - 1, n_sfc)
    first = s * FT
    has_left = s > 0
    has_right = s < n_sfc - 1
    barrier = pltpu.get_barrier_semaphore()

    def greet(gg, ss):
        pl.semaphore_signal(barrier, inc=1, device_id=(gg, ss), device_id_type=MESH)

    for d in (1, 2, 3):
        greet(lax.rem(g + d, 4), s)
    for there, ss in ((has_right, right), (has_left, left)):

        @pl.when(there)
        def _():
            greet(g, ss)

    inside = jnp.logical_and(has_left, has_right)

    def meet():
        pl.when(inside)(lambda: pl.semaphore_wait(barrier, 5))
        pl.when(jnp.logical_not(inside))(lambda: pl.semaphore_wait(barrier, 4))

    class Pair:
        def __init__(self, to_left, to_right):
            self.to_left, self.to_right = to_left, to_right

        def start(self):
            pl.when(has_left)(self.to_left.start)
            pl.when(has_right)(self.to_right.start)

        def wait_recv(self):
            pl.when(has_right)(self.to_left.wait_recv)
            pl.when(has_left)(self.to_right.wait_recv)

        def wait_send(self):
            pl.when(has_left)(self.to_left.wait_send)
            pl.when(has_right)(self.to_right.wait_send)

    def load(source, target, k):
        copy = pltpu.make_async_copy(source, target, ls.at[k])
        copy.start()
        return copy

    def remote(source, target, send, recv, gg, ss):
        return pltpu.make_async_remote_copy(
            src_ref=source, dst_ref=target, send_sem=send, recv_sem=recv,
            device_id=(gg, ss), device_id_type=MESH,
        )

    load_state = load(ff, w0.at[:, HALO : HALO + FT, :], 0)
    load_mean = load(mv, mean, 1)
    load_sound = load(ac, st, 2)

    odd = lax.rem(s, 2) == 1
    even = jnp.logical_not(odd)
    direct_out = {"direct": has_right, "mixed": jnp.logical_and(odd, has_right)}
    direct_in = {"direct": has_left, "mixed": jnp.logical_and(even, has_left)}
    relay_out = {"relay": has_right, "mixed": even}
    relay_in = {"relay": has_left, "mixed": odd}
    mine = pl.ds(pl.multiple_of(SHARE * g, SHARE), SHARE)

    def target(d, h):
        return remote(
            tt, tgt.at[h, g], ts.at[h, d], trs.at[h, g], lax.rem(g + d, 3), right if h else s
        )

    def target_from(q, h):
        return remote(tt, tgt.at[h, q], ts.at[h, 0], trs.at[h, q], lax.rem(g + 1, 3), s)

    def block(turn, part, d, h):
        w = lax.rem(g + d, 3)
        return remote(
            pay.at[turn, part, pl.ds(pl.multiple_of(SHARE * w, SHARE), SHARE), :],
            pb.at[turn, part, h, g], ps.at[turn, part, h, d], prs.at[turn, part, h, g],
            w, right if h else s,
        )

    def block_from(turn, part, q, h):
        return remote(
            pay.at[turn, part, 0:SHARE, :], pb.at[turn, part, h, q],
            ps.at[turn, part, h, 0], prs.at[turn, part, h, q], lax.rem(g + 1, 3), s,
        )

    def passed(turn, part):
        return remote(
            away.at[turn, part], came.at[turn, part],
            ns.at[turn, part], nrs.at[turn, part], g, right,
        )

    def blank_targets():
        @pl.when(jnp.logical_not(has_left))
        def _():
            for q in range(3):
                tgt[1, q] = jnp.full((1, FT), -1, jnp.int32)

    def hot_targets():
        for q in range(3):
            pl.when(g != q)(target_from(q, 0).wait_recv)

        @pl.when(has_left)
        def _():
            for q in range(3):
                target_from(q, 1).wait_recv()

        element = lax.broadcasted_iota(jnp.int32, (EL, FT), 0) + s * EL
        count = jnp.zeros((16, EL), F32)
        ones = jnp.ones((16, FT), BF16)
        for h in range(2):
            for q in range(3):
                order = pltpu.roll(jnp.broadcast_to(tgt[h, q], (8, FT)), 64, 1)[0:1]
                hot = jnp.where(order == element, F32(1.0), F32(0.0)).astype(BF16)
                oht[h, q] = hot
                count = count + dot_t(ones, hot)
                if h == 0:
                    ohn[q] = jnp.where(order == element + EL, F32(1.0), F32(0.0)).astype(BF16)
        return 1.0 / jnp.maximum(count[0:1], 1.0)

    def pass_on(turn, part):
        if ROUTE[turn, part] == "direct":
            return

        @pl.when(relay_out[ROUTE[turn, part]])
        def _():
            cols = slice(128 * part, 128 * part + 128)
            total = sum(dot_t(pb[turn, part, 0, q], ohn[q, :, cols]) for q in range(3))
            away[turn, part] = total.astype(BF16)
            passed(turn, part).start()

    def reduce(turn, inverse):
        for part in (1, 0):
            for q in range(3):
                pl.when(g != q)(block_from(turn, part, q, 0).wait_recv)
            pass_on(turn, part)
        total = jnp.zeros((SHARE, EL), F32)
        for q in range(3):
            total = total + dot_t(
                jnp.concatenate([pb[turn, 0, 0, q], pb[turn, 1, 0, q]], 1), oht[0, q]
            )
        tot[...] = total
        for part in (1, 0):
            route = ROUTE[turn, part]
            if route != "relay":

                @pl.when(direct_in[route])
                def _():
                    more = jnp.zeros((SHARE, EL), F32)
                    for q in range(3):
                        block_from(turn, part, q, 1).wait_recv()
                        cols = slice(128 * part, 128 * part + 128)
                        more = more + dot_t(pb[turn, part, 1, q], oht[1, q, :, cols])
                    tot[...] += more

            if route != "direct":

                @pl.when(relay_in[route])
                def _():
                    passed(turn, part).wait_recv()
                    tot[...] += came[turn, part].astype(F32)

        return (tot[...] * inverse).astype(BF16)

    def passed_sent():
        for (turn, part), route in ROUTE.items():
            if route != "direct":
                pl.when(relay_out[route])(passed(turn, part).wait_send)

    @pl.when(g < 3)
    def _():
        load_visc = load(cv, vis.at[HALO : HALO + FT, :], 3)
        load_links = load(tl, lk.at[0:4, 128 : 128 + FT], 4)
        load_targets = load(tt, tgt.at[0, g], 5)
        load_proj = load(pj, proj, 6)
        load_state.wait()
        load_visc.wait()
        for side, at in ((0, HALO), (1, FT)):
            for f in range(5):
                hb[side, f] = w0[f, at : at + HALO, :].astype(BF16)
            hb[side, 5] = vis[at : at + HALO, :].astype(BF16)
        meet()
        halo = Pair(
            remote(hb.at[0], hn.at[1], hs.at[0], hrs.at[0], g, left),
            remote(hb.at[1], hn.at[0], hs.at[1], hrs.at[1], g, right),
        )
        halo_links = Pair(
            remote(tl.at[:, 0:128], lk.at[0:4, 128 + FT : 256 + FT], hs.at[2], hrs.at[2], g, left),
            remote(tl.at[:, FT - 128 : FT], lk.at[0:4, 0:128], hs.at[3], hrs.at[3], g, right),
        )
        halo.start()
        halo_links.start()
        for there, slot, lanes in ((has_left, 0, slice(0, 128)), (has_right, 1, slice(128 + FT, 256 + FT))):

            @pl.when(jnp.logical_not(there))
            def _():
                hn[slot] = jnp.zeros((6, HALO, CELLS), BF16)
                lk[0:4, lanes] = jnp.zeros((4, 128), jnp.int32)

        for d in (1, 2):
            target(d, 0).start()
        blank_targets()
        lk[4:8, :] = jnp.zeros((4, 2 * 128 + FT), jnp.int32)
        blank = jnp.zeros((HW, CELLS), F32)
        for f in range(5):
            for at in (0, HALO, HALO + FT - HW, WIDE - HW):
                w1[f, at : at + HW, :] = blank

        def select(links, own, shift):
            cols = lax.broadcasted_iota(jnp.int32, (links.shape[0], 256), 1)
            hot = []
            for k in range(4):
                link = links[:, k : k + 1]
                at = jnp.where(link < 0, own, link - shift)
                hot.append(jnp.where(cols == at, F32(1.0), F32(0.0)))
            return (
                (hot[0] + hot[1] + hot[2] + hot[3]).astype(BF16),
                (hot[0] - hot[1]).astype(BF16),
                (hot[2] - hot[3]).astype(BF16),
            )

        def rows_at(ref, k, ranges):
            parts = [ref[k, i:j, :] for i, j in ranges]
            return parts[0] if len(parts) == 1 else jnp.concatenate(parts, 0)

        def gather(rows, window):
            r = dot(rows, jnp.concatenate(halves(window), 1))
            return r[:, :CELLS] + r[:, CELLS:]

        def east_west(c):
            return pltpu.roll(c, CELLS - 1, 1), pltpu.roll(c, 1, 1)

        def advance(source, target, rows, columns, ranges, fields):
            n = sum(j - i for i, j in ranges)
            nu = jnp.concatenate([vis[i:j, :] for i, j in ranges], 0)
            velocity = [rows_at(source, f, ranges) for f in (1, 2, 3)]
            differences = []
            for f in fields:
                c = velocity[f - 1] if 0 < f < 4 else rows_at(source, f, ranges)
                near = gather(rows, rows_at(source, f, columns))
                around, d2, d3_ = near[0:n], near[n : 2 * n], near[2 * n : 3 * n]
                east, west = east_west(c)
                d1 = east - west
                new = (
                    c
                    + nu * (east + west + around - 6.0 * c)
                    - 0.05 * (velocity[0] * d1 + velocity[1] * d2 + velocity[2] * d3_)
                )
                at = 0
                for i, j in ranges:
                    target[f, i:j, :] = new[at : at + j - i]
                    at += j - i
                differences.append((d1, d2, d3_))
            return velocity, differences

        def differ(source, rows, columns, ranges):
            n = sum(j - i for i, j in ranges)
            velocity, differences = [], []
            for f in (1, 2, 3):
                c = rows_at(source, f, ranges)
                near = gather(rows, rows_at(source, f, columns))
                east, west = east_west(c)
                velocity.append(c)
                differences.append((east - west, near[0:n], near[n : 2 * n]))
            return velocity, differences

        def sources(turn, own, velocity, differences):
            (u1, u2, u3), (v1, v2, v3), (w1_, w2_, w3_) = differences
            u, v, w = velocity
            vx = 0.5 * (w2_ - v3)
            vy = 0.5 * (u3 - w1_)
            vz = 0.5 * (v1 - u2)
            packed = [vy * w - vz * v, vz * u - vx * w, vx * v - vy * u]
            for k in range(3):
                m = 0.9 * rows_at(mean, k, own) + 0.1 * velocity[k]
                packed.append(m)
                at = 0
                for i, j in own:
                    mean[k, i:j, :] = m[at : at + j - i]
                    at += j - i
            for k in range(6):
                hi, lo = halves(packed[k])
                at = 0
                for i, j in own:
                    for part, base, x0, x1 in ((0, 64, 0, 64), (1, -64, 64, 192), (0, -192, 192, 256)):
                        lo_, hi_ = max(i, x0), min(j, x1)
                        if lo_ < hi_:
                            rows = slice(at + lo_ - i, at + hi_ - i)
                            to = slice(lo_ + base, hi_ + base)
                            xb[turn, part, k, to, 0:128] = hi[rows]
                            xb[turn, part, k, to, 128:256] = lo[rows]
                    at += j - i

        def project(turn, part):
            for k in range(6):
                x = xb[turn, part, k]
                pay[turn, part, NP * k : NP * (k + 1), :] = (
                    dot_t(p2, x) + dot_t(plow, x[:, 0:128])
                ).astype(BF16)
            pb[turn, part, 0, g] = pay[turn, part, mine, :]

        def send_payload(turn, part):
            for d in (1, 2):
                block(turn, part, d, 0).start()

        def send_next(turn, part):
            if ROUTE[turn, part] != "relay":

                @pl.when(direct_out[ROUTE[turn, part]])
                def _():
                    for d in (1, 2, 0):
                        block(turn, part, d, 1).start()

        load_links.wait()
        mid = HALO + HW, HALO + FT - HW
        n_mid = FT - 2 * HW
        own = lax.broadcasted_iota(jnp.int32, (n_mid, 1), 0) + HW
        links = jnp.transpose(lk[:, 128 : 128 + FT])[HW : FT - HW]
        for m, hot in enumerate(select(links, own, first)):
            sel_mid[m] = hot
        load_proj.wait()
        load_mean.wait()
        ph, plow = halves(proj[...])
        p2 = jnp.concatenate([ph, ph], 1)

        def mid_rows(skip, mats):
            return jnp.concatenate([sel_mid[m, skip : n_mid - skip, :] for m in mats], 0)

        inner = [(HALO, HALO + FT)]
        advance(w0, w1, mid_rows(0, (0, 1, 2)), inner, [mid], (0, 1, 2, 3, 4))
        one = [(mid[0] + HW, mid[1] - HW)]
        velocity, differences = advance(w1, w0, mid_rows(HW, (0, 1, 2)), inner, one, (1, 2, 3))
        sources(0, [(2 * HW, FT - 2 * HW)], velocity, differences)
        project(0, 1)
        send_payload(0, 1)
        two = [(mid[0] + 2 * HW, mid[1] - 2 * HW)]
        velocity, differences = differ(w0, mid_rows(2 * HW, (1, 2)), inner, two)
        sources(1, [(3 * HW, FT - 3 * HW)], velocity, differences)
        project(1, 1)

        halo_links.wait_recv()

        @pl.when(has_right)
        def _():
            for d in range(3):
                target(d, 1).start()

        send_next(0, 1)
        n_end = 5 * HW
        place = lax.broadcasted_iota(jnp.int32, (n_end, 1), 0)
        lt = jnp.transpose(lk[...])
        for side, (at, own_at, shift) in enumerate(
            ((128 - 2 * HW, HW, first - HALO), (128 + FT - HALO, 128 + 2 * HW, first + HALO))
        ):
            for m, hot in enumerate(select(lt[at : at + n_end], place + own_at, shift)):
                sel_end[m, n_end * side : n_end * (side + 1), :] = hot
        halo.wait_recv()
        for side, at in ((0, 0), (1, HALO + FT)):
            for f in range(5):
                w0[f, at : at + HALO, :] = hn[side, f].astype(F32)
            vis[at : at + HALO, :] = hn[side, 5].astype(F32)

        def end_rows(skip, mats):
            parts = []
            for m in mats:
                parts.append(sel_end[m, skip : skip + HALO, :])
                parts.append(sel_end[m, 2 * n_end - HALO - skip : 2 * n_end - skip, :])
            return jnp.concatenate(parts, 0)

        outer = [(0, 128), (WIDE - 128, WIDE)]

        def end_ranges(skip):
            return [(skip, skip + HALO), (WIDE - HALO - skip, WIDE - skip)]

        advance(w0, w1, end_rows(0, (0, 1, 2)), outer, end_ranges(HW), (1, 2, 3, 0, 4))
        velocity, differences = advance(
            w1, w0, end_rows(HW, (0, 1, 2)), outer, end_ranges(2 * HW), (1, 2, 3)
        )
        sources(
            0,
            [(0, 2 * HW), (FT - 2 * HW, FT)],
            [x[HW : HW + 4 * HW] for x in velocity],
            [[x[HW : HW + 4 * HW] for x in d] for d in differences],
        )
        project(0, 0)
        send_payload(0, 0)
        send_next(0, 0)
        send_payload(1, 1)
        send_next(1, 1)
        velocity, differences = differ(w0, end_rows(2 * HW, (1, 2)), outer, end_ranges(3 * HW))
        sources(1, [(0, 3 * HW), (FT - 3 * HW, FT)], velocity, differences)
        project(1, 0)
        send_payload(1, 0)
        send_next(1, 0)
        load_targets.wait()
        inverse = hot_targets()
        for turn in range(TURNS):
            res[turn] = reduce(turn, inverse)
            remote(
                res.at[turn], src.at[turn, mine, :], rs.at[turn], rrs.at[turn, g], 3, s
            ).start()
        advance(w1, w0, mid_rows(HW, (0, 1, 2)), inner, one, (0, 4))
        advance(w1, w0, end_rows(HW, (0, 1, 2)), outer, end_ranges(2 * HW), (0, 4))
        load_sound.wait()
        writes = [
            pltpu.make_async_copy(w0.at[:, HALO : HALO + FT, :], fo, outs.at[0]),
            pltpu.make_async_copy(mean, mo, outs.at[1]),
            pltpu.make_async_copy(st, ao, outs.at[2]),
        ]
        for copy in writes:
            copy.start()

        for turn in range(TURNS):
            remote(
                res.at[turn], src.at[turn, mine, :], rs.at[turn], rrs.at[turn, g], 3, s
            ).wait_send()
            for part in range(2):
                route = ROUTE[turn, part]
                for d in (1, 2):
                    block(turn, part, d, 0).wait_send()
                if route != "relay":

                    @pl.when(direct_out[route])
                    def _():
                        for d in range(3):
                            block(turn, part, d, 1).wait_send()

        passed_sent()
        for d in (1, 2):
            target(d, 0).wait_send()

        @pl.when(has_right)
        def _():
            for d in range(3):
                target(d, 1).wait_send()

        halo.wait_send()
        halo_links.wait_send()
        for copy in writes:
            copy.wait()

    @pl.when(g == 3)
    def _():
        loads = [
            load(en, enb, 3),
            load(fc, fcb, 4),
            load(d3_h, d3, 5),
            load(pick_h, pick, 6),
            load(put_h, put, 7),
        ]
        meet()
        load_sound.wait()

        def send_state(turn):
            for side, at, lanes in ((0, 0, slice(0, 128)), (1, 112, slice(128, 256))):
                packed = jnp.zeros((32, 128), F32)
                for q in range(8):
                    x = st[q // 2, 32 * (q % 2) : 32 * (q % 2) + 32, lanes]
                    packed = jnp.where(group == q, pltpu.roll(x, (HW * q - at) % 128, 1), packed)
                ends[turn, side] = packed.astype(BF16)
            copies = Pair(
                remote(ends.at[turn, 0], hr.at[turn], as_.at[turn, 0], ars.at[turn, 0], 3, left),
                remote(ends.at[turn, 1], hl.at[turn], as_.at[turn, 1], ars.at[turn, 1], 3, right),
            )
            copies.start()
            for there, box in ((has_left, hl), (has_right, hr)):

                @pl.when(jnp.logical_not(there))
                def _():
                    box[turn] = jnp.zeros((32, 128), BF16)

            for v in range(4):
                sb[turn, NP * v : NP * (v + 1), :] = st[v].astype(BF16)
            return copies

        group = lax.broadcasted_iota(jnp.int32, (32, 128), 1) >> 4
        sends = send_state(0)
        load_state.wait()
        load_mean.wait()
        writes = [
            pltpu.make_async_copy(w0.at[:, HALO : HALO + FT, :], fo, outs.at[0]),
            pltpu.make_async_copy(mean, mo, outs.at[1]),
        ]
        for copy in writes:
            copy.start()
        for copy in loads:
            copy.wait()

        row = lax.broadcasted_iota(jnp.int32, (EL + 128, EL), 0)
        for f in range(6):
            link = enb[f]
            at = link - s * EL
            at = jnp.where(link < 0, 999, jnp.where(at < 0, at + (EL + 128), at))
            ohf[f] = jnp.where(row == at, F32(1.0), F32(0.0)).astype(BF16)
        node = lax.broadcasted_iota(jnp.int32, (NP, EL), 0)
        faces_on = jnp.zeros((NP, EL), F32)
        for f in range(6):
            coordinate = (node >> (2 * (f // 2))) & 3
            valid = jnp.where(enb[f] >= 0, F32(1.0), F32(0.0))
            faces_on = faces_on + jnp.where(coordinate == 3 * (f % 2), valid, F32(0.0))

        for turn in range(TURNS):
            for v in range(4):
                hi, lo = halves(st[v])
                grad[v] = dot(d3[...], jnp.concatenate([hi, lo, hi], 0))
            sends.wait_recv()
            sends.wait_send()
            after, before_ = hr[turn].astype(F32), hl[turn].astype(F32)
            beside = jnp.concatenate(
                [
                    jnp.where(
                        group == 0,
                        pltpu.roll(after, (-HW * q) % 128, 1),
                        pltpu.roll(before_, (112 - HW * q) % 128, 1),
                    )
                    for q in range(8)
                ],
                0,
            ).astype(BF16)
            facing = []
            for v in range(4):
                rows = slice(NP * v, NP * (v + 1))
                wide = jnp.concatenate([sb[turn, rows, :], beside[rows]], 1)
                facing.append(dot(pick[...], wide).astype(BF16))
            remotes = []
            for f in range(6):
                stacked = jnp.concatenate([facing[v][16 * f : 16 * f + 16] for v in range(4)], 0)
                remotes.append(dot(stacked, ohf[f]))
            before = []
            for v in range(4):
                turned = []
                for r in range(4):
                    for f in range(6):
                        turned.append(
                            jnp.where(
                                fcb[f] == r, remotes[f][16 * v : 16 * v + 16], F32(0.0)
                            ).astype(BF16)
                        )
                jump = dot(put[...], jnp.concatenate(turned, 0)) - faces_on * st[v]
                if v == 0:
                    linear = grad[1, 0:64] + grad[2, 64:128] + grad[3, 128:192]
                else:
                    linear = grad[0, 64 * (v - 1) : 64 * v]
                before.append(st[v] + 0.08 * (1.5 * jump - linear))
            for w in range(3):
                rows = slice(SHARE * w, SHARE * w + SHARE)
                remote(
                    res.at[turn], src.at[turn, rows, :], rs.at[turn], rrs.at[turn, w], w, s
                ).wait_recv()
            flow = [src[turn, 192 + 64 * d : 256 + 64 * d, :].astype(F32) for d in range(3)]
            for v in range(4):
                convect = sum(flow[d] * grad[v, 64 * d : 64 * d + 64] for d in range(3))
                if v:
                    convect = convect + src[turn, 64 * (v - 1) : 64 * v, :].astype(F32)
                st[v] = before[v] - 0.08 * convect
            if turn == 0:
                sends = send_state(1)
        write = pltpu.make_async_copy(st, ao, outs.at[2])
        write.start()
        for copy in writes:
            copy.wait()
        write.wait()


def store(a, b, c, x, y, z, sems):
    copies = [
        pltpu.make_async_copy(source, target, sems.at[k])
        for k, (source, target) in enumerate(((a, x), (b, y), (c, z)))
    ]
    for copy in copies:
        copy.start()
    for copy in copies:
        copy.wait()


def body(ff, mv, cv, tl, tt, pj, ac, en, fc):
    n_sfc = lax.axis_size("sfc")
    hbm = pl.BlockSpec(memory_space=pltpu.MemorySpace.HBM)
    any_space = pl.BlockSpec(memory_space=pl.ANY)
    dma = pltpu.SemaphoreType.DMA
    outs = pl.pallas_call(
        functools.partial(kernel, n_sfc),
        out_shape=(
            jax.ShapeDtypeStruct((5, FT, CELLS), F32),
            jax.ShapeDtypeStruct((3, FT, CELLS), F32),
            jax.ShapeDtypeStruct((4, NP, EL), F32),
        ),
        in_specs=[hbm] * 12,
        out_specs=(any_space,) * 3,
        scratch_shapes=[
            pltpu.VMEM((5, WIDE, CELLS), F32),
            pltpu.VMEM((5, WIDE, CELLS), F32),
            pltpu.VMEM((WIDE, CELLS), F32),
            pltpu.VMEM((2, 6, HALO, CELLS), BF16),
            pltpu.VMEM((2, 6, HALO, CELLS), BF16),
            pltpu.VMEM((8, 256 + FT), jnp.int32),
            pltpu.VMEM((3, FT, CELLS), F32),
            pltpu.VMEM((3, FT - 2 * HW, 256), BF16),
            pltpu.VMEM((3, 10 * HW, 256), BF16),
            pltpu.VMEM((TURNS, 2, 6, 128, 256), BF16),
            pltpu.VMEM((TURNS, 2, 6 * NP, 128), BF16),
            pltpu.VMEM((2, 3, 1, FT), jnp.int32),
            pltpu.VMEM((2, 3, EL, FT), BF16),
            pltpu.VMEM((3, EL, FT), BF16),
            pltpu.VMEM((TURNS, 2, 2, 3, SHARE, 128), BF16),
            pltpu.VMEM((TURNS, 2, SHARE, EL), BF16),
            pltpu.VMEM((TURNS, 2, SHARE, EL), BF16),
            pltpu.VMEM((SHARE, EL), F32),
            pltpu.VMEM((TURNS, SHARE, EL), BF16),
            pltpu.VMEM((NP, CELLS), F32),
            pltpu.VMEM((4, NP, EL), F32),
            pltpu.VMEM((TURNS, 4 * NP, EL), BF16),
            pltpu.VMEM((TURNS, 2, 32, 128), BF16),
            pltpu.VMEM((TURNS, 32, 128), BF16),
            pltpu.VMEM((TURNS, 32, 128), BF16),
            pltpu.VMEM((6, 1, EL), jnp.int32),
            pltpu.VMEM((6, 1, EL), jnp.int32),
            pltpu.VMEM((192, 192), BF16),
            pltpu.VMEM((96, NP), BF16),
            pltpu.VMEM((NP, 384), BF16),
            pltpu.VMEM((6, EL + 128, EL), BF16),
            pltpu.VMEM((4, 192, EL), F32),
            pltpu.VMEM((TURNS, 6 * NP, EL), BF16),
            dma((8,)),
            dma((4,)), dma((4,)),
            dma((2, 3)), dma((2, 3)),
            dma((TURNS, 2, 2, 3)), dma((TURNS, 2, 2, 3)),
            dma((TURNS, 2)), dma((TURNS, 2)),
            dma((TURNS,)), dma((TURNS, 3)),
            dma((TURNS, 2)), dma((TURNS, 2)),
            dma((3,)),
        ],
        compiler_params=pltpu.CompilerParams(
            collective_id=0, has_side_effects=True, vmem_limit_bytes=48 * 1024 * 1024
        ),
    )(*(
        pltpu.with_memory_space_constraint(x, pltpu.MemorySpace.HBM)
        for x in (
            ff[0], mv[0], cv[0], tl[0], tt, pj, ac[0],
            jnp.swapaxes(en, 0, 1), jnp.swapaxes(fc, 0, 1), *constants(),
        )
    ))
    outs = pl.pallas_call(
        store,
        out_shape=tuple(jax.ShapeDtypeStruct(o.shape, o.dtype) for o in outs),
        in_specs=[any_space] * 3,
        out_specs=(hbm,) * 3,
        scratch_shapes=[dma((3,))],
        compiler_params=pltpu.CompilerParams(vmem_limit_bytes=1024 * 1024),
    )(*outs)
    return tuple(o[None] for o in outs)


def solution(mesh):
    placed = (
        P("grp", None, "sfc", None),
        P("grp", None, "sfc", None),
        P("grp", "sfc", None),
        P("grp", None, "sfc"),
        P("grp", "sfc"),
        P(),
        P("grp", None, None, "sfc"),
        P("grp", None, "sfc"),
        P("grp", None, "sfc"),
    )
    return jax.shard_map(
        body,
        mesh=mesh,
        in_specs=placed,
        out_specs=(
            P("grp", None, "sfc", None),
            P("grp", None, "sfc", None),
            P("grp", None, None, "sfc"),
        ),
        check_vma=False,
    )
```

```python
import functools

import jax
import jax.numpy as jnp
import numpy as np
from jax import lax
from jax.experimental import pallas as pl
from jax.experimental.pallas import tpu as pltpu
from jax.sharding import PartitionSpec as P

MESH = pl.DeviceIdType.MESH
F32 = jnp.float32
BF16 = jnp.bfloat16

HW = 16
FT = 256
CELLS = 128
HALO = 3 * HW
WIDE = FT + 2 * HALO
EL = 256
NP = 64
TURNS = 2
SHARE = 128
ROUTE = {(0, 1): "direct", (0, 0): "direct", (1, 1): "mixed", (1, 0): "direct"}


def derivative_operators():
    points = np.array([-1.0, -1.0 / np.sqrt(5.0), 1.0 / np.sqrt(5.0), 1.0])
    weights = np.array(
        [
            1.0 / np.prod([points[col] - points[other] for other in range(4) if other != col])
            for col in range(4)
        ]
    )
    matrix = np.zeros((4, 4))
    for line in range(4):
        for col in range(4):
            if line != col:
                matrix[line, col] = weights[col] / weights[line] / (points[line] - points[col])
        matrix[line, line] = -matrix[line].sum()
    eye = np.eye(4)
    return np.concatenate(
        [
            np.kron(eye, np.kron(eye, matrix)),
            np.kron(eye, np.kron(matrix, eye)),
            np.kron(matrix, np.kron(eye, eye)),
        ]
    ).astype(np.float32)


def face_tables():
    faces = []
    for face in range(6):
        axis, level = face // 2, 3 * (face % 2)
        members = []
        for second in range(4):
            for first in range(4):
                coords = [first, second]
                coords.insert(axis, level)
                members.append(coords[0] + 4 * coords[1] + 16 * coords[2])
        faces.append(members)
    turns = []
    for turn in range(4):
        mapping = []
        for second in range(4):
            for first in range(4):
                source = ((first, second), (3 - second, first), (3 - first, 3 - second), (second, 3 - first))[turn]
                mapping.append(source[0] + 4 * source[1])
        turns.append(mapping)
    return faces, turns


def constants():
    deriv = jnp.asarray(derivative_operators())
    high = deriv.astype(BF16)
    low = (deriv - high.astype(F32)).astype(BF16)
    deriv3 = jnp.concatenate([high, high, low], 1)
    faces, turns = face_tables()
    pick = np.zeros((96, NP), np.float32)
    put = np.zeros((NP, 4 * 96), np.float32)
    for face in range(6):
        for p in range(16):
            pick[16 * face + p, faces[face ^ 1][p]] = 1
            for turn in range(4):
                put[faces[face][p], 96 * turn + 16 * face + turns[turn][p]] = 1
    return deriv3, jnp.asarray(pick, BF16), jnp.asarray(put, BF16)


def halves(x):
    high = x.astype(BF16)
    return high, (x - high.astype(F32)).astype(BF16)


def dot(a, b):
    return lax.dot_general(a, b, (((1,), (0,)), ((), ())), preferred_element_type=F32)


def dot_t(a, b):
    return lax.dot_general(a, b, (((1,), (1,)), ((), ())), preferred_element_type=F32)


def kernel(
    n_sfc,
    ff, mv, cv, tl, tt, pj, ac, en, fc, d3_h, pick_h, put_h,
    fo, mean, st,
    w0, w1, w2, vis, hb, hn, lk, sel_mid, sel_end, xb, pay, tgt, oht, ohn, pb, away, came, tot, res, proj,
    sb, ends, hl, hr, enb, fcb, d3, pick, put, ohf, ohe, before, grad, src,
    ls, hs, hrs, ts, trs, ps, prs, ns, nrs, rs, rrs, as_, ars, outs,
):
    g = lax.axis_index("grp")
    s = lax.axis_index("sfc")
    right = lax.rem(s + 1, n_sfc)
    left = lax.rem(s + n_sfc - 1, n_sfc)
    first = s * FT
    has_left = s > 0
    has_right = s < n_sfc - 1
    barrier = pltpu.get_barrier_semaphore()

    def greet(gg, ss):
        pl.semaphore_signal(barrier, inc=1, device_id=(gg, ss), device_id_type=MESH)

    for d in (1, 2, 3):
        greet(lax.rem(g + d, 4), s)
    for there, ss in ((has_right, right), (has_left, left)):

        @pl.when(there)
        def _():
            greet(g, ss)

    inside = jnp.logical_and(has_left, has_right)

    def meet():
        pl.when(inside)(lambda: pl.semaphore_wait(barrier, 5))
        pl.when(jnp.logical_not(inside))(lambda: pl.semaphore_wait(barrier, 4))

    class Pair:
        def __init__(self, to_left, to_right):
            self.to_left, self.to_right = to_left, to_right

        def start(self):
            pl.when(has_left)(self.to_left.start)
            pl.when(has_right)(self.to_right.start)

        def wait_recv(self):
            pl.when(has_right)(self.to_left.wait_recv)
            pl.when(has_left)(self.to_right.wait_recv)

        def wait_send(self):
            pl.when(has_left)(self.to_left.wait_send)
            pl.when(has_right)(self.to_right.wait_send)

    def load(source, target, k):
        copy = pltpu.make_async_copy(source, target, ls.at[k])
        copy.start()
        return copy

    def remote(source, target, send, recv, gg, ss):
        return pltpu.make_async_remote_copy(
            src_ref=source, dst_ref=target, send_sem=send, recv_sem=recv,
            device_id=(gg, ss), device_id_type=MESH,
        )

    load_state = load(ff, w0.at[:, HALO : HALO + FT, :], 0)
    load_mean = load(mv, mean, 1)
    load_sound = load(ac, st, 2)

    odd = lax.rem(s, 2) == 1
    even = jnp.logical_not(odd)
    direct_out = {"direct": has_right, "mixed": jnp.logical_and(odd, has_right)}
    direct_in = {"direct": has_left, "mixed": jnp.logical_and(even, has_left)}
    relay_out = {"relay": has_right, "mixed": even}
    relay_in = {"relay": has_left, "mixed": odd}
    mine = pl.ds(pl.multiple_of(SHARE * g, SHARE), SHARE)

    def target(d, h):
        return remote(
            tt, tgt.at[h, g], ts.at[h, d], trs.at[h, g], lax.rem(g + d, 3), right if h else s
        )

    def target_from(q, h):
        return remote(tt, tgt.at[h, q], ts.at[h, 0], trs.at[h, q], lax.rem(g + 1, 3), s)

    def block(turn, part, d, h):
        w = lax.rem(g + d, 3)
        return remote(
            pay.at[turn, part, pl.ds(pl.multiple_of(SHARE * w, SHARE), SHARE), :],
            pb.at[turn, part, h, g], ps.at[turn, part, h, d], prs.at[turn, part, h, g],
            w, right if h else s,
        )

    def block_from(turn, part, q, h):
        return remote(
            pay.at[turn, part, 0:SHARE, :], pb.at[turn, part, h, q],
            ps.at[turn, part, h, 0], prs.at[turn, part, h, q], lax.rem(g + 1, 3), s,
        )

    def passed(turn, part):
        return remote(
            away.at[turn, part], came.at[turn, part],
            ns.at[turn, part], nrs.at[turn, part], g, right,
        )

    def blank_targets():
        @pl.when(jnp.logical_not(has_left))
        def _():
            for q in range(3):
                tgt[1, q] = jnp.full((1, FT), -1, jnp.int32)

    def hot_targets():
        for q in range(3):
            pl.when(g != q)(target_from(q, 0).wait_recv)

        @pl.when(has_left)
        def _():
            for q in range(3):
                target_from(q, 1).wait_recv()

        element = lax.broadcasted_iota(jnp.int32, (EL, FT), 0) + s * EL
        count = jnp.zeros((16, EL), F32)
        ones = jnp.ones((16, FT), BF16)
        for h in range(2):
            for q in range(3):
                order = pltpu.roll(jnp.broadcast_to(tgt[h, q], (8, FT)), 64, 1)[0:1]
                hot = jnp.where(order == element, F32(1.0), F32(0.0)).astype(BF16)
                oht[h, q] = hot
                count = count + dot_t(ones, hot)
                if h == 0:
                    ohn[q] = jnp.where(order == element + EL, F32(1.0), F32(0.0)).astype(BF16)
        return 1.0 / jnp.maximum(count[0:1], 1.0)

    def pass_on(turn, part):
        if ROUTE[turn, part] == "direct":
            return

        @pl.when(relay_out[ROUTE[turn, part]])
        def _():
            cols = slice(128 * part, 128 * part + 128)
            total = sum(dot_t(pb[turn, part, 0, q], ohn[q, :, cols]) for q in range(3))
            away[turn, part] = total.astype(BF16)
            passed(turn, part).start()

    def reduce(turn, inverse):
        for part in (1, 0):
            for q in range(3):
                pl.when(g != q)(block_from(turn, part, q, 0).wait_recv)
            pass_on(turn, part)
        total = jnp.zeros((SHARE, EL), F32)
        for q in range(3):
            total = total + dot_t(
                jnp.concatenate([pb[turn, 0, 0, q], pb[turn, 1, 0, q]], 1), oht[0, q]
            )
        tot[...] = total
        for part in (1, 0):
            route = ROUTE[turn, part]
            if route != "relay":

                @pl.when(direct_in[route])
                def _():
                    more = jnp.zeros((SHARE, EL), F32)
                    for q in range(3):
                        block_from(turn, part, q, 1).wait_recv()
                        cols = slice(128 * part, 128 * part + 128)
                        more = more + dot_t(pb[turn, part, 1, q], oht[1, q, :, cols])
                    tot[...] += more

            if route != "direct":

                @pl.when(relay_in[route])
                def _():
                    passed(turn, part).wait_recv()
                    tot[...] += came[turn, part].astype(F32)

        return (tot[...] * inverse).astype(BF16)

    def passed_sent():
        for (turn, part), route in ROUTE.items():
            if route != "direct":
                pl.when(relay_out[route])(passed(turn, part).wait_send)

    @pl.when(g < 3)
    def _():
        load_visc = load(cv, vis.at[HALO : HALO + FT, :], 3)
        load_links = load(tl, lk.at[0:4, 128 : 128 + FT], 4)
        load_targets = load(tt, tgt.at[0, g], 5)
        load_proj = load(pj, proj, 6)
        load_state.wait()
        load_visc.wait()
        for side, at in ((0, HALO), (1, FT)):
            for f in range(5):
                hb[side, f] = w0[f, at : at + HALO, :].astype(BF16)
            hb[side, 5] = vis[at : at + HALO, :].astype(BF16)
        meet()
        halo = Pair(
            remote(hb.at[0], hn.at[1], hs.at[0], hrs.at[0], g, left),
            remote(hb.at[1], hn.at[0], hs.at[1], hrs.at[1], g, right),
        )
        halo_links = Pair(
            remote(tl.at[:, 0:128], lk.at[0:4, 128 + FT : 256 + FT], hs.at[2], hrs.at[2], g, left),
            remote(tl.at[:, FT - 128 : FT], lk.at[0:4, 0:128], hs.at[3], hrs.at[3], g, right),
        )
        halo.start()
        halo_links.start()
        for there, slot, lanes in ((has_left, 0, slice(0, 128)), (has_right, 1, slice(128 + FT, 256 + FT))):

            @pl.when(jnp.logical_not(there))
            def _():
                hn[slot] = jnp.zeros((6, HALO, CELLS), BF16)
                lk[0:4, lanes] = jnp.zeros((4, 128), jnp.int32)

        for d in (1, 2):
            target(d, 0).start()
        blank_targets()
        lk[4:8, :] = jnp.zeros((4, 2 * 128 + FT), jnp.int32)
        blank = jnp.zeros((HW, CELLS), F32)
        for f in range(5):
            for at in (0, HALO, HALO + FT - HW, WIDE - HW):
                w1[f, at : at + HW, :] = blank
            for at in (0, HW, HALO, HALO + HW, WIDE - 5 * HW, WIDE - 4 * HW, WIDE - 2 * HW, WIDE - HW):
                w2[f, at : at + HW, :] = blank

        def select(links, own, shift):
            cols = lax.broadcasted_iota(jnp.int32, (links.shape[0], 256), 1)
            hot = []
            for k in range(4):
                link = links[:, k : k + 1]
                at = jnp.where(link < 0, own, link - shift)
                hot.append(jnp.where(cols == at, F32(1.0), F32(0.0)))
            return (
                (hot[0] + hot[1] + hot[2] + hot[3]).astype(BF16),
                (hot[0] - hot[1]).astype(BF16),
                (hot[2] - hot[3]).astype(BF16),
            )

        def rows_at(ref, k, ranges):
            parts = [ref[k, i:j, :] for i, j in ranges]
            return parts[0] if len(parts) == 1 else jnp.concatenate(parts, 0)

        def gather(rows, window):
            r = dot(rows, jnp.concatenate(halves(window), 1))
            return r[:, :CELLS] + r[:, CELLS:]

        def east_west(c):
            return pltpu.roll(c, CELLS - 1, 1), pltpu.roll(c, 1, 1)

        def advance(source, target, rows, columns, ranges, fields):
            n = sum(j - i for i, j in ranges)
            nu = jnp.concatenate([vis[i:j, :] for i, j in ranges], 0)
            velocity = [rows_at(source, f, ranges) for f in (1, 2, 3)]
            differences = []
            for f in fields:
                c = velocity[f - 1] if 0 < f < 4 else rows_at(source, f, ranges)
                near = gather(rows, rows_at(source, f, columns))
                around, d2, d3_ = near[0:n], near[n : 2 * n], near[2 * n : 3 * n]
                east, west = east_west(c)
                d1 = east - west
                new = (
                    c
                    + nu * (east + west + around - 6.0 * c)
                    - 0.05 * (velocity[0] * d1 + velocity[1] * d2 + velocity[2] * d3_)
                )
                at = 0
                for i, j in ranges:
                    target[f, i:j, :] = new[at : at + j - i]
                    at += j - i
                differences.append((d1, d2, d3_))
            return velocity, differences

        def differ(source, rows, columns, ranges):
            n = sum(j - i for i, j in ranges)
            velocity, differences = [], []
            for f in (1, 2, 3):
                c = rows_at(source, f, ranges)
                near = gather(rows, rows_at(source, f, columns))
                east, west = east_west(c)
                velocity.append(c)
                differences.append((east - west, near[0:n], near[n : 2 * n]))
            return velocity, differences

        def sources(turn, own, velocity, differences):
            (u1, u2, u3), (v1, v2, v3), (w1_, w2_, w3_) = differences
            u, v, w = velocity
            vx = 0.5 * (w2_ - v3)
            vy = 0.5 * (u3 - w1_)
            vz = 0.5 * (v1 - u2)
            packed = [vy * w - vz * v, vz * u - vx * w, vx * v - vy * u]
            for k in range(3):
                m = 0.9 * rows_at(mean, k, own) + 0.1 * velocity[k]
                packed.append(m)
                at = 0
                for i, j in own:
                    mean[k, i:j, :] = m[at : at + j - i]
                    at += j - i
            for k in range(6):
                hi, lo = halves(packed[k])
                at = 0
                for i, j in own:
                    for part, base, x0, x1 in ((0, 64, 0, 64), (1, -64, 64, 192), (0, -192, 192, 256)):
                        lo_, hi_ = max(i, x0), min(j, x1)
                        if lo_ < hi_:
                            rows = slice(at + lo_ - i, at + hi_ - i)
                            to = slice(lo_ + base, hi_ + base)
                            xb[turn, part, k, to, 0:128] = hi[rows]
                            xb[turn, part, k, to, 128:256] = lo[rows]
                    at += j - i

        def project(turn, part):
            for k in range(6):
                x = xb[turn, part, k]
                pay[turn, part, NP * k : NP * (k + 1), :] = (
                    dot_t(p2, x) + dot_t(plow, x[:, 0:128])
                ).astype(BF16)
            pb[turn, part, 0, g] = pay[turn, part, mine, :]

        def send_payload(turn, part):
            for d in (1, 2):
                block(turn, part, d, 0).start()

        def send_next(turn, part):
            if ROUTE[turn, part] != "relay":

                @pl.when(direct_out[ROUTE[turn, part]])
                def _():
                    for d in (1, 2, 0):
                        block(turn, part, d, 1).start()

        load_links.wait()
        mid = HALO + HW, HALO + FT - HW
        n_mid = FT - 2 * HW
        own = lax.broadcasted_iota(jnp.int32, (n_mid, 1), 0) + HW
        links = jnp.transpose(lk[:, 128 : 128 + FT])[HW : FT - HW]
        for m, hot in enumerate(select(links, own, first)):
            sel_mid[m] = hot
        load_proj.wait()
        load_mean.wait()
        ph, plow = halves(proj[...])
        p2 = jnp.concatenate([ph, ph], 1)

        def mid_rows(skip, mats):
            return jnp.concatenate([sel_mid[m, skip : n_mid - skip, :] for m in mats], 0)

        inner = [(HALO, HALO + FT)]
        advance(w0, w1, mid_rows(0, (0, 1, 2)), inner, [mid], (1, 2, 3))
        one = [(mid[0] + HW, mid[1] - HW)]
        velocity, differences = advance(w1, w2, mid_rows(HW, (0, 1, 2)), inner, one, (1, 2, 3))
        sources(0, [(2 * HW, FT - 2 * HW)], velocity, differences)
        project(0, 1)
        send_payload(0, 1)
        two = [(mid[0] + 2 * HW, mid[1] - 2 * HW)]
        velocity, differences = differ(w2, mid_rows(2 * HW, (1, 2)), inner, two)
        sources(1, [(3 * HW, FT - 3 * HW)], velocity, differences)
        project(1, 1)

        halo_links.wait_recv()

        @pl.when(has_right)
        def _():
            for d in range(3):
                target(d, 1).start()

        send_next(0, 1)
        n_end = 5 * HW
        place = lax.broadcasted_iota(jnp.int32, (n_end, 1), 0)
        lt = jnp.transpose(lk[...])
        for side, (at, own_at, shift) in enumerate(
            ((128 - 2 * HW, HW, first - HALO), (128 + FT - HALO, 128 + 2 * HW, first + HALO))
        ):
            for m, hot in enumerate(select(lt[at : at + n_end], place + own_at, shift)):
                sel_end[m, n_end * side : n_end * (side + 1), :] = hot
        halo.wait_recv()
        for side, at in ((0, 0), (1, HALO + FT)):
            for f in range(5):
                w0[f, at : at + HALO, :] = hn[side, f].astype(F32)
            vis[at : at + HALO, :] = hn[side, 5].astype(F32)

        def end_rows(skip, mats):
            parts = []
            for m in mats:
                parts.append(sel_end[m, skip : skip + HALO, :])
                parts.append(sel_end[m, 2 * n_end - HALO - skip : 2 * n_end - skip, :])
            return jnp.concatenate(parts, 0)

        outer = [(0, 128), (WIDE - 128, WIDE)]

        def end_ranges(skip):
            return [(skip, skip + HALO), (WIDE - HALO - skip, WIDE - skip)]

        advance(w0, w1, end_rows(0, (0, 1, 2)), outer, end_ranges(HW), (1, 2, 3))
        velocity, differences = advance(
            w1, w2, end_rows(HW, (0, 1, 2)), outer, end_ranges(2 * HW), (1, 2, 3)
        )
        sources(
            0,
            [(0, 2 * HW), (FT - 2 * HW, FT)],
            [x[HW : HW + 4 * HW] for x in velocity],
            [[x[HW : HW + 4 * HW] for x in d] for d in differences],
        )
        project(0, 0)
        pl.when(odd)(lambda: send_next(0, 0))
        send_payload(0, 0)
        pl.when(even)(lambda: send_next(0, 0))
        send_next(1, 1)
        send_payload(1, 1)
        velocity, differences = differ(w2, end_rows(2 * HW, (1, 2)), outer, end_ranges(3 * HW))
        sources(1, [(0, 3 * HW), (FT - 3 * HW, FT)], velocity, differences)
        project(1, 0)
        pl.when(odd)(lambda: send_next(1, 0))
        send_payload(1, 0)
        pl.when(even)(lambda: send_next(1, 0))
        load_targets.wait()
        inverse = hot_targets()
        for turn in range(TURNS):
            res[turn] = reduce(turn, inverse)
            remote(
                res.at[turn], src.at[turn, mine, :], rs.at[turn], rrs.at[turn, g], 3, s
            ).start()
            if turn == 0:
                advance(w0, w1, mid_rows(0, (0, 1, 2)), inner, [mid], (0, 4))
                advance(w0, w1, end_rows(0, (0, 1, 2)), outer, end_ranges(HW), (0, 4))
        advance(w1, w2, mid_rows(HW, (0, 1, 2)), inner, one, (0, 4))
        advance(w1, w2, end_rows(HW, (0, 1, 2)), outer, end_ranges(2 * HW), (0, 4))
        load_sound.wait()
        writes = [
            pltpu.make_async_copy(w2.at[:, HALO : HALO + FT, :], fo, outs.at[0]),
        ]
        for copy in writes:
            copy.start()

        for turn in range(TURNS):
            remote(
                res.at[turn], src.at[turn, mine, :], rs.at[turn], rrs.at[turn, g], 3, s
            ).wait_send()
            for part in range(2):
                route = ROUTE[turn, part]
                for d in (1, 2):
                    block(turn, part, d, 0).wait_send()
                if route != "relay":

                    @pl.when(direct_out[route])
                    def _():
                        for d in range(3):
                            block(turn, part, d, 1).wait_send()

        passed_sent()
        for d in (1, 2):
            target(d, 0).wait_send()

        @pl.when(has_right)
        def _():
            for d in range(3):
                target(d, 1).wait_send()

        halo.wait_send()
        halo_links.wait_send()
        for copy in writes:
            copy.wait()

    @pl.when(g == 3)
    def _():
        loads = [
            load(en, enb, 3),
            load(fc, fcb, 4),
            load(d3_h, d3, 5),
            load(pick_h, pick, 6),
            load(put_h, put, 7),
        ]
        meet()
        load_sound.wait()

        def send_state(turn):
            for side, at, lanes in ((0, 0, slice(0, 128)), (1, 112, slice(128, 256))):
                packed = jnp.zeros((32, 128), F32)
                for q in range(8):
                    x = st[q // 2, 32 * (q % 2) : 32 * (q % 2) + 32, lanes]
                    packed = jnp.where(group == q, pltpu.roll(x, (HW * q - at) % 128, 1), packed)
                ends[turn, side] = packed.astype(BF16)
            copies = Pair(
                remote(ends.at[turn, 0], hr.at[turn], as_.at[turn, 0], ars.at[turn, 0], 3, left),
                remote(ends.at[turn, 1], hl.at[turn], as_.at[turn, 1], ars.at[turn, 1], 3, right),
            )
            copies.start()
            for there, box in ((has_left, hl), (has_right, hr)):

                @pl.when(jnp.logical_not(there))
                def _():
                    box[turn] = jnp.zeros((32, 128), BF16)

            for v in range(4):
                sb[turn, NP * v : NP * (v + 1), :] = st[v].astype(BF16)
            return copies

        group = lax.broadcasted_iota(jnp.int32, (32, 128), 1) >> 4
        sends = send_state(0)
        load_state.wait()
        load_mean.wait()
        writes = [
            pltpu.make_async_copy(w0.at[:, HALO : HALO + FT, :], fo, outs.at[0]),
        ]
        for copy in writes:
            copy.start()
        for copy in loads:
            copy.wait()

        row = lax.broadcasted_iota(jnp.int32, (EL, EL), 0)
        edge_row = lax.broadcasted_iota(jnp.int32, (128, 128), 0)
        low = lax.broadcasted_iota(jnp.int32, (1, 128), 1) < 64

        def edges(x):
            return jnp.where(low, x[:, 0:128], x[:, 128:256])

        for f in range(6):
            link = enb[f]
            at = jnp.where(link < 0, 999, link - s * EL)
            ohf[f] = jnp.where(row == at, F32(1.0), F32(0.0)).astype(BF16)
            at = edges(at)
            at = jnp.where(at < 0, at + 128, jnp.where(at < EL, 999, at - EL))
            ohe[f] = jnp.where(edge_row == at, F32(1.0), F32(0.0)).astype(BF16)
        node = lax.broadcasted_iota(jnp.int32, (NP, EL), 0)
        faces_on = jnp.zeros((NP, EL), F32)
        for f in range(6):
            coordinate = (node >> (2 * (f // 2))) & 3
            valid = jnp.where(enb[f] >= 0, F32(1.0), F32(0.0))
            faces_on = faces_on + jnp.where(coordinate == 3 * (f % 2), valid, F32(0.0))

        for turn in range(TURNS):
            for v in range(4):
                hi, lo = halves(st[v])
                grad[v] = dot(d3[...], jnp.concatenate([hi, lo, hi], 0))

            def jumps(facing, hot, code):
                remotes = []
                for f in range(6):
                    stacked = jnp.concatenate(
                        [facing[v][16 * f : 16 * f + 16] for v in range(4)], 0
                    )
                    remotes.append(dot(stacked, hot[f]))
                out = []
                for v in range(4):
                    turned = [
                        jnp.where(
                            code(f) == r, remotes[f][16 * v : 16 * v + 16], F32(0.0)
                        ).astype(BF16)
                        for r in range(4)
                        for f in range(6)
                    ]
                    out.append(dot(put[...], jnp.concatenate(turned, 0)))
                return out

            facing = [
                dot(pick[...], sb[turn, NP * v : NP * (v + 1), :]).astype(BF16) for v in range(4)
            ]
            within = jumps(facing, ohf, lambda f: fcb[f])
            for v in range(4):
                if v == 0:
                    linear = grad[1, 0:64] + grad[2, 64:128] + grad[3, 128:192]
                else:
                    linear = grad[0, 64 * (v - 1) : 64 * v]
                before[v] = st[v] + 0.08 * (1.5 * (within[v] - faces_on * st[v]) - linear)
            sends.wait_recv()
            sends.wait_send()
            after, before_ = hr[turn].astype(F32), hl[turn].astype(F32)
            beside = jnp.concatenate(
                [
                    jnp.where(
                        group == 0,
                        pltpu.roll(after, (-HW * q) % 128, 1),
                        pltpu.roll(before_, (112 - HW * q) % 128, 1),
                    )
                    for q in range(8)
                ],
                0,
            ).astype(BF16)
            facing = [
                dot(pick[...], beside[NP * v : NP * (v + 1)]).astype(BF16) for v in range(4)
            ]
            across = jumps(facing, ohe, lambda f: edges(fcb[f]))
            for v in range(4):
                added = 0.08 * 1.5 * across[v]
                before[v, :, 0:128] += jnp.where(low, added, F32(0.0))
                before[v, :, 128:256] += jnp.where(low, F32(0.0), added)
            for w in range(3):
                rows = slice(SHARE * w, SHARE * w + SHARE)
                remote(
                    res.at[turn], src.at[turn, rows, :], rs.at[turn], rrs.at[turn, w], w, s
                ).wait_recv()
            flow = [src[turn, 192 + 64 * d : 256 + 64 * d, :].astype(F32) for d in range(3)]
            for v in range(4):
                convect = sum(flow[d] * grad[v, 64 * d : 64 * d + 64] for d in range(3))
                if v:
                    convect = convect + src[turn, 64 * (v - 1) : 64 * v, :].astype(F32)
                st[v] = before[v] - 0.08 * convect
            if turn == 0:
                sends = send_state(1)
        for copy in writes:
            copy.wait()


def store(a, b, c, x, y, z, sems):
    copies = [
        pltpu.make_async_copy(source, target, sems.at[k])
        for k, (source, target) in enumerate(((a, x), (b, y), (c, z)))
    ]
    for copy in copies:
        copy.start()
    for copy in copies:
        copy.wait()


def body(ff, mv, cv, tl, tt, pj, ac, en, fc):
    n_sfc = lax.axis_size("sfc")
    hbm = pl.BlockSpec(memory_space=pltpu.MemorySpace.HBM)
    any_space = pl.BlockSpec(memory_space=pl.ANY)
    vmem = pl.BlockSpec(memory_space=pltpu.MemorySpace.VMEM)
    dma = pltpu.SemaphoreType.DMA
    outs = pl.pallas_call(
        functools.partial(kernel, n_sfc),
        out_shape=(
            jax.ShapeDtypeStruct((5, FT, CELLS), F32),
            jax.ShapeDtypeStruct((3, FT, CELLS), F32),
            jax.ShapeDtypeStruct((4, NP, EL), F32),
        ),
        in_specs=[hbm] * 12,
        out_specs=(any_space, vmem, vmem),
        scratch_shapes=[
            pltpu.VMEM((5, WIDE, CELLS), F32),
            pltpu.VMEM((5, WIDE, CELLS), F32),
            pltpu.VMEM((5, WIDE, CELLS), F32),
            pltpu.VMEM((WIDE, CELLS), F32),
            pltpu.VMEM((2, 6, HALO, CELLS), BF16),
            pltpu.VMEM((2, 6, HALO, CELLS), BF16),
            pltpu.VMEM((8, 256 + FT), jnp.int32),
            pltpu.VMEM((3, FT - 2 * HW, 256), BF16),
            pltpu.VMEM((3, 10 * HW, 256), BF16),
            pltpu.VMEM((TURNS, 2, 6, 128, 256), BF16),
            pltpu.VMEM((TURNS, 2, 6 * NP, 128), BF16),
            pltpu.VMEM((2, 3, 1, FT), jnp.int32),
            pltpu.VMEM((2, 3, EL, FT), BF16),
            pltpu.VMEM((3, EL, FT), BF16),
            pltpu.VMEM((TURNS, 2, 2, 3, SHARE, 128), BF16),
            pltpu.VMEM((TURNS, 2, SHARE, EL), BF16),
            pltpu.VMEM((TURNS, 2, SHARE, EL), BF16),
            pltpu.VMEM((SHARE, EL), F32),
            pltpu.VMEM((TURNS, SHARE, EL), BF16),
            pltpu.VMEM((NP, CELLS), F32),
            pltpu.VMEM((TURNS, 4 * NP, EL), BF16),
            pltpu.VMEM((TURNS, 2, 32, 128), BF16),
            pltpu.VMEM((TURNS, 32, 128), BF16),
            pltpu.VMEM((TURNS, 32, 128), BF16),
            pltpu.VMEM((6, 1, EL), jnp.int32),
            pltpu.VMEM((6, 1, EL), jnp.int32),
            pltpu.VMEM((192, 192), BF16),
            pltpu.VMEM((96, NP), BF16),
            pltpu.VMEM((NP, 384), BF16),
            pltpu.VMEM((6, EL, EL), BF16),
            pltpu.VMEM((6, 128, 128), BF16),
            pltpu.VMEM((4, NP, EL), F32),
            pltpu.VMEM((4, 192, EL), F32),
            pltpu.VMEM((TURNS, 6 * NP, EL), BF16),
            dma((8,)),
            dma((4,)), dma((4,)),
            dma((2, 3)), dma((2, 3)),
            dma((TURNS, 2, 2, 3)), dma((TURNS, 2, 2, 3)),
            dma((TURNS, 2)), dma((TURNS, 2)),
            dma((TURNS,)), dma((TURNS, 3)),
            dma((TURNS, 2)), dma((TURNS, 2)),
            dma((1,)),
        ],
        compiler_params=pltpu.CompilerParams(
            collective_id=0, has_side_effects=True, vmem_limit_bytes=48 * 1024 * 1024
        ),
    )(*(
        pltpu.with_memory_space_constraint(x, pltpu.MemorySpace.HBM)
        for x in (
            ff[0], mv[0], cv[0], tl[0], tt, pj, ac[0],
            jnp.swapaxes(en, 0, 1), jnp.swapaxes(fc, 0, 1), *constants(),
        )
    ))
    outs = pl.pallas_call(
        store,
        out_shape=tuple(jax.ShapeDtypeStruct(o.shape, o.dtype) for o in outs),
        in_specs=[any_space] * 3,
        out_specs=(hbm,) * 3,
        scratch_shapes=[dma((3,))],
        compiler_params=pltpu.CompilerParams(vmem_limit_bytes=1024 * 1024),
    )(*outs)
    return tuple(o[None] for o in outs)


def solution(mesh):
    placed = (
        P("grp", None, "sfc", None),
        P("grp", None, "sfc", None),
        P("grp", "sfc", None),
        P("grp", None, "sfc"),
        P("grp", "sfc"),
        P(),
        P("grp", None, None, "sfc"),
        P("grp", None, "sfc"),
        P("grp", None, "sfc"),
    )
    return jax.shard_map(
        body,
        mesh=mesh,
        in_specs=placed,
        out_specs=(
            P("grp", None, "sfc", None),
            P("grp", None, "sfc", None),
            P("grp", None, None, "sfc"),
        ),
        check_vma=False,
    )
```
